32 devices in a mesh: layer: 2 (over x), latent: 4 (over y, core), token: 4 (over z).
Axes of the slice: x: 2, y: 2, z: 4, core: 2. Of those that a mesh axis runs over, the one named last changes fastest.
Arguments:
- resid_in: bfloat16 [2, 1024, 2304], P('layer', 'token', 'latent'), may hold values from -300 to 300
- clt_gain: float32 [2, 2304], P('layer'), may hold values from 0.1 to 1.9
- enc_w: bfloat16 [2, 2304, 16384], P('layer', None, 'latent'), may hold values from -0.125 to 0.125
- enc_b: float32 [2, 16384], P('layer', 'latent'), may hold values from -3 to 3
- dec_same: bfloat16 [2, 16384, 2304], P('layer', 'latent'), may hold values from -0.0625 to 0.0625
- dec_next: bfloat16 [16384, 2304], P('latent'), may hold values from -0.0625 to 0.0625
- frozen_sum: bfloat16 [1024, 2304], P('token', 'latent'), may hold values from -300 to 300
- mlp_gain: float32 [2304], P('latent'), may hold values from 0.1 to 1.9
- w_gate: bfloat16 [2304, 9216], P(None, ('layer', 'latent')), may hold values from -0.125 to 0.125
- w_up: bfloat16 [2304, 9216], P(None, ('layer', 'latent')), may hold values from -0.125 to 0.125
- w_down: bfloat16 [9216, 2304], P(('layer', 'latent')), may hold values from -0.09375 to 0.09375
Outputs:
- latents: bfloat16 [2, 1024, 16384], P('layer', 'token', 'latent')
- recon: bfloat16 [2, 1024, 2304], P('layer', 'token', 'latent')
- mlp_out: bfloat16 [1024, 2304], P('token', ('layer', 'latent'))
The draws below stay inside these ranges and needn't reach their ends.
All inputs are finite; a program needn't handle non-finite values.
Results may differ from the reference program's by a relative error of at most 0.0074.
Values may be sent and summed in bfloat16 or wider, within the bound.
No kernel may reach another device: no remote copies, remote signals or barrier semaphores. Data moves between devices by JAX's collectives and lax.ppermute only.
A program may use at most 128 MiB of HBM per device.

```python
import math
import jax
import jax.numpy as jnp
from jax import lax

D = 2304
HID = 9216
FEAT = 16384
LAYERS = 2
TOKENS = 1024


def scaled_field(key, row_count, col_count, salt, low, high):
    key = jax.random.fold_in(key, salt)
    key_rows, key_cols, key_base = jax.random.split(key, 3)
    row_scale = jnp.exp(jax.random.uniform(key_rows, (row_count, 1), jnp.float32, math.log(low), math.log(high)))
    ramp = jnp.exp(math.log(4.0) * jnp.arange(col_count, dtype=jnp.float32) / (col_count - 1))
    jitter = jnp.exp(jax.random.uniform(key_cols, (col_count,), jnp.float32, math.log(0.6), math.log(1.5)))
    base = jnp.clip(jax.random.normal(key_base, (row_count, col_count), jnp.float32), -4.0, 4.0)
    return base * row_scale * ramp * jitter


def draw_resid_in(key, part):
    field = scaled_field(key, LAYERS * TOKENS, D, 11, 0.5, 8.0)
    return field.reshape(LAYERS, TOKENS, D).astype(jnp.bfloat16)


def draw_frozen_sum(key, part):
    return scaled_field(key, TOKENS, D, 23, 0.3, 3.0).astype(jnp.bfloat16)


def spiked(array, own_key, source, target, shards_of, factor):
    def block_of(axis_at):
        return (jnp.arange(array.shape[axis_at]) // (array.shape[axis_at] // shards_of)).reshape((-1,) + (1,) * (array.ndim - 1 - axis_at))

    near = jax.random.permutation(own_key, shards_of)[block_of(target)]
    second = (block_of(target) + shards_of // 2) % shards_of
    return jnp.where((block_of(source) == near) | (block_of(source) == second), factor * array, array)


def block_levels(own_key, extent, cuts, least, top_value):
    gain = 1.0
    for position, shards_of in cuts:
        draws = jax.random.uniform(jax.random.fold_in(jax.random.fold_in(own_key, 6), position), (shards_of,), jnp.float32, least / len(cuts), top_value / len(cuts))
        gain = gain * jnp.repeat(jnp.exp(draws), extent[position] // shards_of).reshape((-1,) + (1,) * (len(extent) - 1 - position))
    return gain


def bell_draw(own_key, shape, spread, most, shards=(), kind=jnp.bfloat16):
    values = jax.random.normal(own_key, shape, jnp.float32) * spread
    if len(shards) > 0:
        values = block_levels(own_key, shape, shards, -0.22, 0.18) * values
    return jnp.clip(values, min=-most, max=most).astype(kind)


def heavy_noise(stream_key, dims, spread, limit, cuts, heavy, kind=jnp.bfloat16):
    drawn = spread * jax.random.normal(stream_key, dims, jnp.float32)
    if cuts:
        drawn = drawn * block_levels(stream_key, dims, cuts, -0.22, 0.18)
    return jnp.clip(spiked(drawn, jax.random.fold_in(stream_key, 3), *heavy), -limit, limit).astype(kind)


def setup_inputs(seed: int = 0) -> dict:
    arg_keys = jax.random.split(jax.random.key(seed), 12)
    resid_in = draw_resid_in(jax.random.fold_in(arg_keys[11], 71), 0)
    clt_gain = jnp.clip(1.0 + 0.18 * jax.random.normal(arg_keys[1], (LAYERS, D), jnp.float32), 0.1, 1.9)
    enc_w = bell_draw(arg_keys[2], (LAYERS, D, FEAT), D ** -0.5, 0.125, ((0, 2), (2, 4)))
    enc_b = bell_draw(arg_keys[3], (LAYERS, FEAT), 0.5, 3.0, ((0, 2), (1, 4)), jnp.float32)
    dec_same = heavy_noise(arg_keys[4], (LAYERS, FEAT, D), FEAT ** -0.5, 0.0625, ((0, 2), (1, 4)), (1, 2, 4, 2.0))
    dec_next = heavy_noise(arg_keys[5], (FEAT, D), FEAT ** -0.5, 0.0625, ((0, 4),), (0, 1, 4, 2.0))
    frozen_sum = draw_frozen_sum(jax.random.fold_in(arg_keys[11], 71), 0)
    mlp_gain = jnp.clip(1.0 + 0.18 * jax.random.normal(arg_keys[7], (D,), jnp.float32), 0.1, 1.9)
    w_gate = bell_draw(arg_keys[8], (D, HID), D ** -0.5, 0.125, ((1, 8),))
    w_up = bell_draw(arg_keys[9], (D, HID), D ** -0.5, 0.125, ((1, 8),))
    w_down = heavy_noise(arg_keys[10], (HID, D), HID ** -0.5, 0.09375, ((0, 8),), (0, 1, 8, 2.0))
    return {"resid_in": resid_in, "clt_gain": clt_gain, "enc_w": enc_w, "enc_b": enc_b, "dec_same": dec_same, "dec_next": dec_next, "frozen_sum": frozen_sum, "mlp_gain": mlp_gain, "w_gate": w_gate, "w_up": w_up, "w_down": w_down}


def inv_rms(values):
    return lax.rsqrt(lax.optimization_barrier(jnp.mean(values * values, axis=-1, keepdims=True)) + 1e-06)

def reference(resid_in, clt_gain, enc_w, enc_b, dec_same, dec_next, frozen_sum, mlp_gain, w_gate, w_up, w_down):
    layer_lats = []
    for source in range(LAYERS):
        values = resid_in[source].astype(jnp.float32)
        gated = (values * clt_gain[source]).astype(jnp.bfloat16)
        pre_act = inv_rms(values) * jnp.dot(gated, enc_w[source], preferred_element_type=jnp.float32) + enc_b[source]
        layer_lats.append(jnp.maximum(pre_act, 0.0).astype(jnp.bfloat16))
    recon_zero = jnp.dot(layer_lats[0], dec_same[0], preferred_element_type=jnp.float32)
    recon_one = jnp.dot(layer_lats[0], dec_next, preferred_element_type=jnp.float32) + jnp.dot(layer_lats[1], dec_same[1], preferred_element_type=jnp.float32)
    recon = jnp.stack([recon_zero, recon_one]).astype(jnp.bfloat16)
    mixed = frozen_sum.astype(jnp.float32) + recon_zero + recon_one
    normed = (mixed * mlp_gain).astype(jnp.bfloat16)
    scale_rows = inv_rms(mixed)
    gate_pre = scale_rows * jnp.dot(normed, w_gate, preferred_element_type=jnp.float32)
    up_pre = scale_rows * jnp.dot(normed, w_up, preferred_element_type=jnp.float32)
    hidden = (jax.nn.gelu(gate_pre, approximate=True) * up_pre).astype(jnp.bfloat16)
    mlp_out = jnp.dot(hidden, w_down, preferred_element_type=jnp.float32).astype(jnp.bfloat16)
    return (jnp.stack(layer_lats), recon, mlp_out)
```

```python
import functools

import jax
import jax.numpy as jnp
from jax import lax
from jax.experimental import pallas as pl
from jax.experimental.pallas import tpu as pltpu
from jax.sharding import PartitionSpec as P

BF = jnp.bfloat16
F32 = jnp.float32
VMEM = pl.BlockSpec(memory_space=pltpu.VMEM)
SMEM = pl.BlockSpec(memory_space=pltpu.SMEM)
HBM = pl.BlockSpec(memory_space=pl.ANY)
TAIL = 16


def dot_cols(x_km, w_kn):
    return lax.dot_general(x_km, w_kn, (((0,), (0,)), ((), ())), preferred_element_type=F32)


def column_of(row, width):
    n = row.shape[1]
    block = jnp.broadcast_to(row, (128, n)).T
    return jnp.concatenate([block] * (width // 128), axis=1)


def call(kernel, out_shapes, scratch, args, specs, name, out_specs=None):
    return pl.pallas_call(
        kernel,
        out_shape=out_shapes,
        in_specs=specs,
        out_specs=[VMEM] * len(out_shapes) if out_specs is None else out_specs,
        scratch_shapes=scratch,
        name=name,
        compiler_params=pltpu.CompilerParams(vmem_limit_bytes=52 << 20),
    )(*args)


def pick(total, wanted):
    size = wanted - wanted % 128
    while size > 128 and total % size:
        size -= 128
    return size if total % size == 0 else total


def encode_half(ids, own, other, gain, enc, first, extra):
    width, tokens = own.shape
    feats, lats = enc.shape
    half = 2 * width
    tn = pick(lats, 1024)
    steps = lats // tn
    last = not first

    def kernel(ids_ref, own_ref, other_ref, gain_ref, enc_ref, *rest):
        if first:
            acc_ref, sq_ref, xg, wbuf, sems = rest
        else:
            acc_in, sq_in, bias_ref, out_ref, xg, wbuf, sems = rest
        core, row = ids_ref[0], ids_ref[1] if first else 1 - ids_ref[1]
        row = pl.multiple_of(row * half, half)

        def copy(j):
            cols = pl.ds(j * tn, tn)
            return pltpu.make_async_copy(enc_ref.at[pl.ds(row, half), cols], wbuf.at[:, cols], sems.at[j])

        for j in range(steps):
            copy(j).start()
        xg[pl.ds(pl.multiple_of(core * width, width), width), :] = own_ref[...]
        xg[pl.ds(pl.multiple_of((1 - core) * width, width), width), :] = other_ref[...]
        values = xg[...].astype(F32)
        squares = jnp.sum(values * values, axis=0, keepdims=True)
        gains = column_of(gain_ref[:, pl.ds(row, half)], tokens)
        xg[...] = (values * gains).astype(BF)
        if first:
            sq_ref[...] = jnp.broadcast_to(squares, sq_ref.shape)
        else:
            total = squares + sq_in[0:1, :]
            scale = jnp.broadcast_to(lax.rsqrt(total / feats + 1e-06), (128, tokens)).T[:, 0:1]
        for j in range(steps):
            copy(j).wait()
            cols = pl.ds(j * tn, tn)
            part = dot_cols(xg[...], wbuf[:, cols])
            if first:
                acc_ref[:, cols] = part
            else:
                pre = scale * (part + acc_in[:, cols]) + bias_ref[:, cols]
                out_ref[:, cols] = jnp.maximum(pre, 0.0).astype(BF)

    scratch = [
        pltpu.VMEM((half, tokens), BF),
        pltpu.VMEM((half, lats), BF),
        pltpu.SemaphoreType.DMA((steps,)),
    ]
    shape = jax.ShapeDtypeStruct
    if first:
        outs = [shape((tokens, lats), F32), shape((8, tokens), F32)]
    else:
        outs = [shape((tokens, lats), BF)]
    specs = [SMEM, VMEM, VMEM, VMEM, HBM] + [VMEM] * len(extra)
    return call(kernel, outs, scratch, (ids, own, other, gain, enc) + extra, specs, "enc_last" if last else "enc_first")


def decode(ids, lat, dec, only_first, name):
    tokens, lats = lat.shape
    feats = dec.shape[1]
    block = feats // 4
    tn = pick(feats, 768)
    tk = pick(lats, 1024)
    nn, nk = feats // tn, lats // tk

    def kernel(ids_ref, lat_ref, dec_ref, snd_ref, oth_ref, own_ref, wbuf, yt, sems):
        core, half, layer = ids_ref[0], ids_ref[1], ids_ref[2]

        def copy(n, k):
            at = (pl.ds(k * tk, tk), pl.ds(n * tn, tn))
            return pltpu.make_async_copy(dec_ref.at[at], wbuf.at[at], sems.at[n, k])

        def work():
            for n in range(nn):
                for k in range(nk):
                    copy(n, k).start()
            for n in range(nn):
                acc = None
                for k in range(nk):
                    copy(n, k).wait()
                    part = jnp.dot(
                        lat_ref[:, pl.ds(k * tk, tk)],
                        wbuf[pl.ds(k * tk, tk), pl.ds(n * tn, tn)],
                        preferred_element_type=F32,
                    )
                    acc = part if acc is None else acc + part
                yt[pl.ds(n * tn, tn), :] = acc.T

            def rows(h, c):
                return pl.ds(pl.multiple_of((2 * h + c) * block, block), block)

            snd_ref[0] = yt[rows(1 - half, 1 - core), :].astype(BF)
            snd_ref[1] = yt[rows(half, 1 - core), :].astype(BF)
            oth_ref[...] = yt[rows(1 - half, core), :]
            own_ref[...] = yt[rows(half, core), :]

        if only_first:
            pl.when(layer == 0)(work)
        else:
            work()

    shape = jax.ShapeDtypeStruct
    outs = [shape((2, block, tokens), BF), shape((block, tokens), F32), shape((block, tokens), F32)]
    scratch = [
        pltpu.VMEM((lats, feats), BF),
        pltpu.VMEM((feats, tokens), F32),
        pltpu.SemaphoreType.DMA((nn, nk)),
    ]
    return call(kernel, outs, scratch, (ids, lat, dec), [SMEM, VMEM, HBM], name)


def mix(target, other, frozen, gain):
    block, tokens = target.shape

    def kernel(t_ref, o_ref, f_ref, g_ref, out_ref):
        mixed = f_ref[...].astype(F32) + t_ref[...] + o_ref[...].astype(F32)
        out_ref[pl.ds(0, block), :] = (mixed * g_ref[...]).astype(BF)
        squares = jnp.sum(mixed * mixed, axis=0, keepdims=True)
        high = squares.astype(BF).astype(F32)
        rest = squares - high
        mid = rest.astype(BF).astype(F32)
        low = rest - mid
        row = lax.broadcasted_iota(jnp.int32, (TAIL, tokens), 0)
        tail = jnp.where(row == 0, high, jnp.where(row == 1, mid, jnp.where(row == 2, low, 0.0)))
        out_ref[pl.ds(block, TAIL), :] = tail.astype(BF)

    outs = [jax.ShapeDtypeStruct((block + TAIL, tokens), BF)]
    return call(kernel, outs, [], (target, other, frozen, gain), [VMEM] * 4, "mix")[0]


def mlp_half(ids, own, other, w_gate, w_up, first, extra, layers):
    width, tokens = own.shape[0] - TAIL, own.shape[1]
    half = 2 * width
    feats, units = w_gate.shape
    last = not first
    piece = feats // (4 * layers)
    tn = pick(feats, 768)

    def kernel(ids_ref, own_ref, other_ref, wg_ref, wu_ref, *rest):
        if first:
            g_ref, u_ref, sq_ref, xg, gbuf, ubuf, sems = rest
        else:
            g_in, u_in, sq_in, wd_ref, snd_ref, keep_ref, xg, gbuf, ubuf, sems, dbuf, yt, dsems = rest
        core, side = ids_ref[0], ids_ref[1]
        row = side if first else 1 - side
        row = pl.multiple_of(row * half, half)
        cg = pltpu.make_async_copy(wg_ref.at[pl.ds(row, half), :], gbuf, sems.at[0])
        cu = pltpu.make_async_copy(wu_ref.at[pl.ds(row, half), :], ubuf, sems.at[1])
        cg.start()
        cu.start()
        if last:
            downs = [
                pltpu.make_async_copy(wd_ref.at[:, pl.ds(n * tn, tn)], dbuf.at[:, pl.ds(n * tn, tn)], dsems.at[n])
                for n in range(feats // tn)
            ]
            for d in downs:
                d.start()
        xg[pl.ds(pl.multiple_of(core * width, width), width), :] = own_ref[pl.ds(0, width), :]
        xg[pl.ds(pl.multiple_of((1 - core) * width, width), width), :] = other_ref[pl.ds(0, width), :]
        tails = own_ref[pl.ds(width, TAIL), :].astype(F32) + other_ref[pl.ds(width, TAIL), :].astype(F32)
        squares = jnp.sum(tails, axis=0, keepdims=True)
        cg.wait()
        gate = dot_cols(xg[...], gbuf[...])
        cu.wait()
        up = dot_cols(xg[...], ubuf[...])
        if first:
            g_ref[...] = gate
            u_ref[...] = up
            sq_ref[...] = jnp.broadcast_to(squares, sq_ref.shape)
            return
        total = squares + sq_in[0:1, :]
        scale = jnp.broadcast_to(lax.rsqrt(total / feats + 1e-06), (128, tokens)).T[:, 0:1]
        gate = scale * (gate + g_in[...])
        up = scale * (up + u_in[...])
        hidden = (jax.nn.gelu(gate, approximate=True) * up).astype(BF)
        for n, d in enumerate(downs):
            d.wait()
            yt[pl.ds(n * tn, tn), :] = jnp.dot(hidden, dbuf[:, pl.ds(n * tn, tn)], preferred_element_type=F32).T
        layer = ids_ref[2]
        for i in range(4):
            at = ((layer ^ (i >> 1)) * 2 + (side ^ (i & 1))) * 2
            snd_ref[i] = yt[pl.ds(pl.multiple_of((at + 1 - core) * piece, piece), piece), :].astype(BF)
            keep_ref[i] = yt[pl.ds(pl.multiple_of((at + core) * piece, piece), piece), :]

    shape = jax.ShapeDtypeStruct
    scratch = [
        pltpu.VMEM((half, tokens), BF),
        pltpu.VMEM((half, units), BF),
        pltpu.VMEM((half, units), BF),
        pltpu.SemaphoreType.DMA((2,)),
    ]
    specs = [SMEM, VMEM, VMEM, HBM, HBM]
    if first:
        outs = [shape((tokens, units), F32), shape((tokens, units), F32), shape((8, tokens), F32)]
    else:
        outs = [shape((4, piece, tokens), BF), shape((4, piece, tokens), F32)]
        scratch += [
            pltpu.VMEM((units, feats), BF),
            pltpu.VMEM((feats, tokens), F32),
            pltpu.SemaphoreType.DMA((feats // tn,)),
        ]
        specs += [VMEM, VMEM, VMEM, HBM]
    return call(kernel, outs, scratch, (ids, own, other, w_gate, w_up) + extra, specs, "mlp_last" if last else "mlp_first")


def blocked(
    resid_in, clt_gain, enc_w, enc_b, dec_same, dec_next, frozen_sum, mlp_gain, w_gate, w_up, w_down
):
    layers = lax.axis_size("layer")
    both = ("layer", "latent")
    place = lax.axis_index("latent")
    layer = lax.axis_index("layer")
    ids = jnp.stack([place % 2, place // 2, layer, place]).astype(jnp.int32)

    def partner(v):
        return lax.ppermute(v, "latent", [(i, i ^ 1) for i in range(4)])

    def across(v):
        return lax.ppermute(v, "latent", [(i, i ^ 2) for i in range(4)])

    def other_layer(v):
        return lax.ppermute(v, "layer", [(0, 1), (1, 0)])

    def diagonal(v):
        return lax.ppermute(v, both, [(i, i ^ 6) for i in range(8)])

    own = resid_in[0].T
    far = across(own)
    near = partner(own)
    acc, sq = encode_half(ids, own, near, clt_gain, enc_w[0], True, ())
    far_near = partner(far)
    (lat,) = encode_half(ids, far, far_near, clt_gain, enc_w[0], False, (acc, sq, enc_b))

    def reduced(snd, oth, keep, pairs):
        got = lax.ppermute(snd, both, [(i, i ^ 1) for i in pairs])
        sent = (oth + got[0].astype(F32)).astype(BF)
        back = lax.ppermute(sent, both, [(i, i ^ 2) for i in pairs])
        return keep + got[1].astype(F32) + back.astype(F32)

    q_sum = reduced(*decode(ids, lat, dec_next, True, "dec_next"), range(4))
    q_here = lax.ppermute(q_sum.astype(BF), "layer", [(0, 1)])
    target = reduced(*decode(ids, lat, dec_same[0], False, "dec_same"), range(8)) + q_here.astype(F32)
    target_bf = target.astype(BF)
    swapped = other_layer(target_bf)
    gain = jnp.broadcast_to(mlp_gain[:, None], target.shape)
    normed = mix(target, swapped, frozen_sum.T, gain)
    n_far = across(normed)
    n_near = partner(normed)
    g, u, nsq = mlp_half(ids, normed, n_near, w_gate, w_up, True, (), layers)
    n_far_near = partner(n_far)
    snd, keep = mlp_half(ids, n_far, n_far_near, w_gate, w_up, False, (g, u, nsq, w_down), layers)
    got = partner(snd)
    sums = keep + got.astype(F32)
    sent = sums.astype(BF)
    r_d = diagonal(sent[3])
    r_x = other_layer(sent[2])
    r_y = across(sent[1])
    out = (sums[0] + r_d.astype(F32) + r_x.astype(F32) + r_y.astype(F32)).astype(BF)
    return (lat[None], target_bf.T[None], out.T)


def passed_along(block, axis, distance):
    devices = range(lax.axis_size(axis))
    route = [(i - distance, i) for i in devices if i - distance in devices]
    return lax.ppermute(block, axis, route)


def swapped_with(value, axis, stride):
    mask = 2**stride
    pairs = [(source, source ^ mask) for source in range(lax.axis_size(axis))]
    return lax.ppermute(value, axis, pairs)


def general(
    resid_in, clt_gain, enc_w, enc_b, dec_same, dec_next, frozen_sum, mlp_gain, w_gate, w_up, w_down
):
    own_rows = resid_in[0]
    feats = enc_w.shape[1]
    own_values = own_rows.astype(F32)
    squares = lax.psum(jnp.sum(own_values * own_values, axis=1, keepdims=True), "latent")
    gated = (lax.all_gather(own_rows, "latent", axis=1, tiled=True).astype(F32) * clt_gain[0]).astype(BF)
    projected = jnp.dot(gated, enc_w[0], preferred_element_type=F32)
    inv_scale = lax.rsqrt(squares / feats + 1e-06)
    lat_act = jnp.maximum(inv_scale * projected + enc_b[0], 0.0).astype(BF)
    is_first = lax.axis_index("layer") == 0
    own_term = jnp.dot(lat_act, dec_same[0], preferred_element_type=F32)
    arrived = passed_along(lat_act, "layer", 1)
    target_term = own_term + jnp.dot(arrived, dec_next, preferred_element_type=F32)
    own_sum = lax.psum_scatter(target_term, "latent", scatter_dimension=1, tiled=True)
    other_sum = swapped_with(own_sum, "layer", 0)
    recon_zero = jnp.where(is_first, own_sum, other_sum)
    recon_one = jnp.where(is_first, other_sum, own_sum)
    recon = own_sum.astype(BF)[None]
    mixed = frozen_sum.astype(F32) + recon_zero + recon_one
    normed = (mixed * mlp_gain).astype(BF)
    mixed_squares = lax.psum(jnp.sum(mixed * mixed, axis=1, keepdims=True), "latent")
    rows = lax.all_gather(normed, "latent", axis=1, tiled=True)
    gate_raw = jnp.dot(rows, w_gate, preferred_element_type=F32)
    up_raw = jnp.dot(rows, w_up, preferred_element_type=F32)
    row_scale = lax.rsqrt(mixed_squares / feats + 1e-06)
    hidden = (jax.nn.gelu(row_scale * gate_raw, approximate=True) * (row_scale * up_raw)).astype(BF)
    partials = jnp.dot(hidden, w_down, preferred_element_type=F32)
    mlp_out = lax.psum_scatter(
        partials, ("layer", "latent"), scatter_dimension=1, tiled=True
    ).astype(BF)
    return (lat_act[None], recon, mlp_out)


def solution(mesh):
    in_specs = (
        P("layer", "token", "latent"),
        P("layer", None),
        P("layer", None, "latent"),
        P("layer", "latent"),
        P("layer", "latent", None),
        P("latent", None),
        P("token", "latent"),
        P("latent"),
        P(None, ("layer", "latent")),
        P(None, ("layer", "latent")),
        P(("layer", "latent"), None),
    )
    out_specs = (
        P("layer", "token", "latent"),
        P("layer", "token", "latent"),
        P("token", ("layer", "latent")),
    )
    small = mesh.shape["layer"] == 2 and mesh.shape["latent"] == 4
    return jax.shard_map(
        blocked if small else general, mesh=mesh, in_specs=in_specs, out_specs=out_specs, check_vma=False
    )
```

```python
import jax
import jax.numpy as jnp
from jax import lax
from jax.experimental import pallas as pl
from jax.experimental.pallas import tpu as pltpu
from jax.sharding import PartitionSpec as P


BF = jnp.bfloat16
F32 = jnp.float32
VMEM = pl.BlockSpec(memory_space=pltpu.VMEM)
SMEM = pl.BlockSpec(memory_space=pltpu.SMEM)
HBM = pl.BlockSpec(memory_space=pltpu.HBM)
ANY = pl.BlockSpec(memory_space=pl.ANY)
TAIL = 16


def dot_cols(x_km, w_kn):
    return lax.dot_general(x_km, w_kn, (((0,), (0,)), ((), ())), preferred_element_type=F32)


def column_of(row, width):
    n = row.shape[1]
    block = jnp.broadcast_to(row, (128, n)).T
    return jnp.concatenate([block] * (width // 128), axis=1)


def call(kernel, out_shapes, scratch, args, specs, flops, limit, out_specs=None):
    return pl.pallas_call(
        kernel,
        out_shape=out_shapes,
        in_specs=specs,
        out_specs=[VMEM] * len(out_shapes) if out_specs is None else out_specs,
        scratch_shapes=scratch,
        cost_estimate=pl.CostEstimate(flops=2 * flops, transcendentals=0, bytes_accessed=0),
        compiler_params=pltpu.CompilerParams(vmem_limit_bytes=limit << 20),
    )(*args)


def in_hbm(array):
    return pltpu.with_memory_space_constraint(array, pltpu.HBM)


def resident(weights):
    return pltpu.with_memory_space_constraint(weights, pltpu.VMEM)


def pick(total, wanted):
    size = wanted - wanted % 128
    while size > 128 and total % size:
        size -= 128
    return size if total % size == 0 else total


def encode_first(ids, own, other, gain, bias, mlp_gain, enc):
    width, tokens = own.shape
    _, lats = enc.shape
    half = 2 * width
    tn = pick(lats, 1024)
    steps = lats // tn
    ahead = 3

    def kernel(
        ids_ref, own_ref, other_ref, gain_ref, bias_ref, mlp_ref, enc_ref,
        acc_ref, sq_ref, gain_out, bias_out, rest_ref, mlp_out,
        xg, xown, gbuf, wbuf, sems, small
    ):
        core, side = ids_ref[0], ids_ref[1]
        mine = pl.multiple_of(side * half, half)
        others = pl.multiple_of((1 - side) * half, half)
        loads = [
            pltpu.make_async_copy(own_ref, xown, small.at[0]),
            pltpu.make_async_copy(gain_ref.at[:, pl.ds(mine, half)], gbuf, small.at[1]),
        ]
        later = [
            pltpu.make_async_copy(gain_ref.at[:, pl.ds(others, half)], gain_out, small.at[2]),
            pltpu.make_async_copy(bias_ref, bias_out, small.at[3]),
            pltpu.make_async_copy(mlp_ref, mlp_out, small.at[4]),
        ]

        def weights(j):
            cols = pl.ds(j % steps * tn, tn)
            if j < steps:
                return pltpu.make_async_copy(enc_ref.at[pl.ds(mine, half), cols], wbuf.at[:, cols], sems.at[j])
            return pltpu.make_async_copy(enc_ref.at[pl.ds(others, half), cols], rest_ref.at[:, cols], sems.at[j])

        for c in loads:
            c.start()
        for j in range(ahead):
            weights(j).start()
        for c in later:
            c.start()
        for c in loads:
            c.wait()
        xg[pl.ds(pl.multiple_of(core * width, width), width), :] = xown[...]
        xg[pl.ds(pl.multiple_of((1 - core) * width, width), width), :] = other_ref[...]
        values = xg[...].astype(F32)
        squares = jnp.sum(values * values, axis=0, keepdims=True)
        xg[...] = (values * column_of(gbuf[...], tokens)).astype(BF)
        sq_ref[...] = jnp.broadcast_to(squares, sq_ref.shape)
        for j in range(2 * steps):
            weights(j).wait()
            if j + ahead < 2 * steps:
                weights(j + ahead).start()
            if j < steps:
                cols = pl.ds(j * tn, tn)
                acc_ref[:, cols] = dot_cols(xg[...], wbuf[:, cols])
        for c in later:
            c.wait()

    shape = jax.ShapeDtypeStruct
    outs = [
        shape((tokens, lats), F32),
        shape((8, tokens), F32),
        shape((1, half), F32),
        shape((1, lats), F32),
        shape((half, lats), BF),
        shape(mlp_gain.shape, F32),
    ]
    scratch = [
        pltpu.VMEM((half, tokens), BF),
        pltpu.VMEM((width, tokens), BF),
        pltpu.VMEM((1, half), F32),
        pltpu.VMEM((half, lats), BF),
        pltpu.SemaphoreType.DMA((2 * steps,)),
        pltpu.SemaphoreType.DMA((5,)),
    ]
    specs = [SMEM, HBM, VMEM, HBM, HBM, HBM, HBM]
    return call(
        kernel,
        outs,
        scratch,
        (ids, in_hbm(own), other, in_hbm(gain), in_hbm(bias), in_hbm(mlp_gain), in_hbm(enc)),
        specs,
        4 * tokens * half * lats,
        16,
    )


def encode_last(ids, own, other, acc, sq, gain, bias, rest, feats, dec, ahead):
    width, tokens = own.shape
    half, lats = rest.shape
    tn = pick(lats, 1024)
    steps = lats // tn

    def kernel(
        ids_ref, own_ref, other_ref, acc_ref, sq_ref, gain_ref, bias_ref, rest_ref, dec_ref,
        lat_ref, out_ref, head_ref, xg, sems
    ):
        core = ids_ref[0]
        load = pltpu.make_async_copy(dec_ref.at[:, pl.ds(0, ahead)], head_ref, sems.at[steps])
        load.start()
        xg[pl.ds(pl.multiple_of(core * width, width), width), :] = own_ref[...]
        xg[pl.ds(pl.multiple_of((1 - core) * width, width), width), :] = other_ref[...]
        values = xg[...].astype(F32)
        squares = jnp.sum(values * values, axis=0, keepdims=True) + sq_ref[0:1, :]
        xg[...] = (values * column_of(gain_ref[...], tokens)).astype(BF)
        scale = jnp.broadcast_to(lax.rsqrt(squares / feats + 1e-06), (128, tokens)).T[:, 0:1]
        writes = []
        for j in range(steps):
            cols = pl.ds(j * tn, tn)
            pre = scale * (dot_cols(xg[...], rest_ref[:, cols]) + acc_ref[:, cols]) + bias_ref[:, cols]
            lat_ref[:, cols] = jnp.maximum(pre, 0.0).astype(BF)
            writes.append(pltpu.make_async_copy(lat_ref.at[:, cols], out_ref.at[:, cols], sems.at[j]))
            writes[-1].start()
        for c in writes + [load]:
            c.wait()

    shape = jax.ShapeDtypeStruct((tokens, lats), BF)
    scratch = [pltpu.VMEM((half, tokens), BF), pltpu.SemaphoreType.DMA((steps + 1,))]
    args = (ids, own, other, acc, sq, gain, bias, rest, in_hbm(dec))
    specs = [SMEM] + [VMEM] * 7 + [HBM]
    outs = [shape, shape, jax.ShapeDtypeStruct((dec.shape[0], ahead), BF)]
    return call(kernel, outs, scratch, args, specs, 2 * tokens * half * lats, 8, [VMEM, HBM, VMEM])


def chunks(start, total):
    sizes, left = [], total - start
    for size in (768, 512):
        while left - size >= 256:
            sizes.append(size)
            left -= size
            if size == 768 and left <= 768:
                break
    if left:
        sizes.append(left)
    at, out = start, []
    for size in sizes:
        out.append((at, size))
        at += size
    return out


def decode(ids, lat, head, dec, after, only_first, loads=()):
    tokens, lats = lat.shape
    feats = dec.shape[1]
    start = head.shape[1]
    block = feats // 4
    tails = chunks(start, feats)
    rows_of = lats // 2

    def kernel(ids_ref, lat_ref, after_ref, head_ref, dec_ref, *rest):
        load_refs, rest = rest[: len(loads)], rest[len(loads) :]
        snd_ref, oth_ref, own_ref, *rest = rest
        loaded_refs, (wbuf, yt, wsems, sems) = rest[: len(loads)], rest[len(loads) :]
        copies = [
            pltpu.make_async_copy(source.at[:, pl.ds(0, cols)], target, sems.at[i])
            for i, (source, target, (_, cols)) in enumerate(zip(load_refs, loaded_refs, loads))
        ]
        core, side, layer = ids_ref[0], ids_ref[1], ids_ref[2]

        def weights(i):
            at, size = tails[i]
            return [
                pltpu.make_async_copy(
                    dec_ref.at[pl.ds(k * rows_of, rows_of), pl.ds(at, size)],
                    wbuf.at[pl.ds(k * rows_of, rows_of), pl.ds(at - start, size)],
                    wsems.at[i, k],
                )
                for k in range(2)
            ]

        def rows(h, c):
            return pl.ds(pl.multiple_of((2 * h + c) * block, block), block)

        def work():
            for i in range(min(2, len(tails))):
                for c in weights(i):
                    c.start()
            yt[pl.ds(0, start), :] = jnp.dot(lat_ref[...], head_ref[...], preferred_element_type=F32).T
            for i, (at, size) in enumerate(tails):
                for c in weights(i):
                    c.wait()
                if i + 2 < len(tails):
                    for c in weights(i + 2):
                        c.start()
                if i + 2 == max(2, len(tails) - 1):
                    for c in copies:
                        c.start()
                part = jnp.dot(lat_ref[...], wbuf[:, pl.ds(at - start, size)], preferred_element_type=F32)
                yt[pl.ds(at, size), :] = part.T
            snd_ref[0] = yt[rows(1 - side, 1 - core), :].astype(BF)
            snd_ref[1] = yt[rows(side, 1 - core), :].astype(BF)
            oth_ref[...] = yt[rows(1 - side, core), :]
            own_ref[...] = yt[rows(side, core), :]

        if only_first:
            pl.when(layer == 0)(work)

            @pl.when(layer != 0)
            def _():
                for c in copies:
                    c.start()
        else:
            work()
        for c in copies:
            c.wait()

    shape = jax.ShapeDtypeStruct
    outs = [shape((2, block, tokens), BF), shape((block, tokens), F32), shape((block, tokens), F32)]
    outs += [shape((v.shape[0], cols), v.dtype) for v, cols in loads]
    scratch = [
        pltpu.VMEM((lats, feats - start), BF),
        pltpu.VMEM((feats, tokens), F32),
        pltpu.SemaphoreType.DMA((len(tails), 2)),
        pltpu.SemaphoreType.DMA((max(1, len(loads)),)),
    ]
    args = (ids, lat, after, head, in_hbm(dec)) + tuple(in_hbm(v) for v, _ in loads)
    specs = [SMEM, VMEM, ANY, VMEM, HBM] + [HBM] * len(loads)
    return call(kernel, outs, scratch, args, specs, 2 * tokens * lats * feats, 20)


def send_sum(oth, got):
    def kernel(oth_ref, got_ref, out_ref):
        out_ref[...] = (oth_ref[...] + got_ref[0].astype(F32)).astype(BF)

    outs = [jax.ShapeDtypeStruct(oth.shape, BF)]
    return call(kernel, outs, [], (oth, got), [VMEM] * 2, oth.size, 4)[0]


def own_sum(own, got, back):
    def kernel(own_ref, got_ref, back_ref, out_ref):
        out_ref[...] = (own_ref[...] + got_ref[1].astype(F32) + back_ref[...].astype(F32)).astype(BF)

    outs = [jax.ShapeDtypeStruct(own.shape, BF)]
    return call(kernel, outs, [], (own, got, back), [VMEM] * 3, own.size, 4)[0]


def target_sum(own, got, back, extra):
    def kernel(own_ref, got_ref, back_ref, extra_ref, sum_ref, out_ref):
        total = own_ref[...] + got_ref[1].astype(F32) + back_ref[...].astype(F32) + extra_ref[...].astype(F32)
        sum_ref[...] = total
        out_ref[...] = total.astype(BF)

    outs = [jax.ShapeDtypeStruct(own.shape, F32), jax.ShapeDtypeStruct(own.shape, BF)]
    return call(kernel, outs, [], (own, got, back, extra), [VMEM] * 4, own.size, 5)


def last_sum(own, *others):
    def kernel(own_ref, *refs):
        *other_refs, out_ref = refs
        total = own_ref[...]
        for r in other_refs:
            total = total + r[...].astype(F32)
        out_ref[...] = total.astype(BF)

    outs = [jax.ShapeDtypeStruct(own.shape, BF)]
    return call(kernel, outs, [], (own,) + others, [VMEM] * (1 + len(others)), own.size, 4)[0]


def mix(target, other, frozen, gain):
    block, tokens = target.shape

    def kernel(t_ref, o_ref, f_ref, g_ref, out_ref):
        mixed = f_ref[...].astype(F32) + t_ref[...] + o_ref[...].astype(F32)
        out_ref[pl.ds(0, block), :] = (mixed * column_of(g_ref[...], tokens)).astype(BF)
        squares = jnp.sum(mixed * mixed, axis=0, keepdims=True)
        high = squares.astype(BF).astype(F32)
        rest = squares - high
        mid = rest.astype(BF).astype(F32)
        low = rest - mid
        row = lax.broadcasted_iota(jnp.int32, (TAIL, tokens), 0)
        tail = jnp.where(row == 0, high, jnp.where(row == 1, mid, jnp.where(row == 2, low, 0.0)))
        out_ref[pl.ds(block, TAIL), :] = tail.astype(BF)

    outs = [jax.ShapeDtypeStruct((block + TAIL, tokens), BF)]
    return call(kernel, outs, [], (target, other, frozen, gain), [VMEM] * 4, block * tokens, 5)[0]


def fold(keep, got):
    count, piece, tokens = keep.shape

    def kernel(keep_ref, got_ref, own_ref, *sent):
        own_ref[...] = keep_ref[0] + got_ref[0].astype(F32)
        for i in range(1, count):
            sent[i - 1][...] = (keep_ref[i] + got_ref[i].astype(F32)).astype(BF)

    shape = jax.ShapeDtypeStruct
    outs = [shape((piece, tokens), F32)] + [shape((piece, tokens), BF)] * (count - 1)
    return call(kernel, outs, [], (keep, got), [VMEM] * 2, count * piece * tokens, 6)


def mlp_half(ids, own, other, w_gate, w_up, first, extra, layers):
    width, tokens = own.shape[0] - TAIL, own.shape[1]
    half = 2 * width
    feats, units = w_gate.shape
    piece = feats // (4 * layers)
    tn = pick(feats, 768)

    def kernel(ids_ref, own_ref, other_ref, wg_ref, wu_ref, *rest):
        if first:
            g_ref, u_ref, sq_ref, xg = rest
        else:
            g_in, u_in, sq_in, wd_ref, snd_ref, keep_ref, xg, yt = rest
        core, side = ids_ref[0], ids_ref[1]
        row = side if first else 1 - side
        row = pl.multiple_of(row * half, half)
        xg[pl.ds(pl.multiple_of(core * width, width), width), :] = own_ref[pl.ds(0, width), :]
        xg[pl.ds(pl.multiple_of((1 - core) * width, width), width), :] = other_ref[pl.ds(0, width), :]
        tails = own_ref[pl.ds(width, TAIL), :].astype(F32) + other_ref[pl.ds(width, TAIL), :].astype(F32)
        squares = jnp.sum(tails, axis=0, keepdims=True)
        gate = dot_cols(xg[...], wg_ref[pl.ds(row, half), :])
        up = dot_cols(xg[...], wu_ref[pl.ds(row, half), :])
        if first:
            g_ref[...] = gate
            u_ref[...] = up
            sq_ref[...] = jnp.broadcast_to(squares, sq_ref.shape)
            return
        total = squares + sq_in[0:1, :]
        scale = jnp.broadcast_to(lax.rsqrt(total / feats + 1e-06), (128, tokens)).T[:, 0:1]
        gate = scale * (gate + g_in[...])
        up = scale * (up + u_in[...])
        hidden = (jax.nn.gelu(gate, approximate=True) * up).astype(BF)
        for n in range(feats // tn):
            cols = pl.ds(n * tn, tn)
            yt[cols, :] = jnp.dot(hidden, wd_ref[:, cols], preferred_element_type=F32).T
        layer = ids_ref[2]
        for i in range(4):
            at = ((layer ^ (i >> 1)) * 2 + (side ^ (i & 1))) * 2
            snd_ref[i] = yt[pl.ds(pl.multiple_of((at + 1 - core) * piece, piece), piece), :].astype(BF)
            keep_ref[i] = yt[pl.ds(pl.multiple_of((at + core) * piece, piece), piece), :]

    shape = jax.ShapeDtypeStruct
    scratch = [pltpu.VMEM((half, tokens), BF)]
    if first:
        outs = [shape((tokens, units), F32), shape((tokens, units), F32), shape((8, tokens), F32)]
    else:
        outs = [shape((4, piece, tokens), BF), shape((4, piece, tokens), F32)]
        scratch += [pltpu.VMEM((feats, tokens), F32)]
    args = (ids, own, other, w_gate, w_up) + extra
    flops = 4 * tokens * half * units + (0 if first else 2 * tokens * units * feats)
    return call(kernel, outs, scratch, args, [SMEM] + [VMEM] * (len(args) - 1), flops, 6 if first else 12)


def blocked(
    resid_in, clt_gain, enc_w, enc_b, dec_same, dec_next, frozen_sum, mlp_gain, w_gate, w_up, w_down
):
    return blocked_steps(
        resid_in, clt_gain, enc_w, enc_b, dec_same, dec_next, frozen_sum, mlp_gain, w_gate, w_up, w_down
    )


def blocked_steps(
    resid_in, clt_gain, enc_w, enc_b, dec_same, dec_next, frozen_sum, mlp_gain, w_gate, w_up, w_down
):
    layers = lax.axis_size("layer")
    both = ("layer", "latent")
    place = lax.axis_index("latent")
    layer = lax.axis_index("layer")
    ids = jnp.stack([place & 1, place >> 1, layer]).astype(jnp.int32)

    def partner(v):
        return lax.ppermute(v, "latent", [(i, i ^ 1) for i in range(4)])

    def across(v):
        return lax.ppermute(v, "latent", [(i, i ^ 2) for i in range(4)])

    def other_layer(v):
        return lax.ppermute(v, "layer", [(0, 1), (1, 0)])

    own = resid_in[0].T
    far = across(own)
    near = partner(own)
    *parts, gain = encode_first(ids, own, near, clt_gain, enc_b, mlp_gain[None], enc_w[0])
    far_near = partner(far)
    ahead = pick(dec_next.shape[1], 768)
    lat, lat_out, head = encode_last(ids, far, far_near, *parts, enc_w.shape[1], dec_next, ahead)

    def reduced(head, dec, after, only_first, pairs, loads):
        snd, oth, own, *loaded = decode(ids, lat, head, dec, after, only_first, loads)
        got = lax.ppermute(snd, both, [(i, i ^ 1) for i in pairs])
        back = lax.ppermute(send_sum(oth, got), both, [(i, i ^ 2) for i in pairs])
        return own, got, back, snd, loaded

    same, frozen = dec_same[0], frozen_sum.T
    *q_parts, after, (head,) = reduced(head, dec_next, lat, True, range(4), ((same, ahead),))
    q_here = lax.ppermute(own_sum(*q_parts), "layer", [(0, 1)])
    *p_parts, _, (frozen,) = reduced(head, same, after, False, range(8), ((frozen, frozen.shape[1]),))
    target, target_bf = target_sum(*p_parts, q_here)
    swapped = other_layer(target_bf)
    normed = mix(target, swapped, frozen, gain)
    w_gate, w_up, w_down = resident(w_gate), resident(w_up), resident(w_down)
    n_far = across(normed)
    n_near = partner(normed)
    g, u, nsq = mlp_half(ids, normed, n_near, w_gate, w_up, True, (), layers)
    n_far_near = partner(n_far)
    snd, keep = mlp_half(ids, n_far, n_far_near, w_gate, w_up, False, (g, u, nsq, w_down), layers)
    got = partner(snd)
    kept, to_y, to_x, to_d = fold(keep, got)
    r_d = lax.ppermute(to_d, both, [(i, i ^ 6) for i in range(8)])
    r_x = other_layer(to_x)
    r_y = across(to_y)
    out = last_sum(kept, r_x, r_y, r_d)
    return (lat_out[None], target_bf.T[None], out.T)


def passed_along(block, axis, distance):
    devices = range(lax.axis_size(axis))
    route = [(i - distance, i) for i in devices if i - distance in devices]
    return lax.ppermute(block, axis, route)


def swapped_with(value, axis, stride):
    mask = 2**stride
    pairs = [(source, source ^ mask) for source in range(lax.axis_size(axis))]
    return lax.ppermute(value, axis, pairs)


def general(
    resid_in, clt_gain, enc_w, enc_b, dec_same, dec_next, frozen_sum, mlp_gain, w_gate, w_up, w_down
):
    own_rows = resid_in[0]
    feats = enc_w.shape[1]
    own_values = own_rows.astype(F32)
    squares = lax.psum(jnp.sum(own_values * own_values, axis=1, keepdims=True), "latent")
    gated = (lax.all_gather(own_rows, "latent", axis=1, tiled=True).astype(F32) * clt_gain[0]).astype(BF)
    projected = jnp.dot(gated, enc_w[0], preferred_element_type=F32)
    inv_scale = lax.rsqrt(squares / feats + 1e-06)
    lat_act = jnp.maximum(inv_scale * projected + enc_b[0], 0.0).astype(BF)
    is_first = lax.axis_index("layer") == 0
    own_term = jnp.dot(lat_act, dec_same[0], preferred_element_type=F32)
    arrived = passed_along(lat_act, "layer", 1)
    target_term = own_term + jnp.dot(arrived, dec_next, preferred_element_type=F32)
    own_sum = lax.psum_scatter(target_term, "latent", scatter_dimension=1, tiled=True)
    other_sum = swapped_with(own_sum, "layer", 0)
    recon_zero = jnp.where(is_first, own_sum, other_sum)
    recon_one = jnp.where(is_first, other_sum, own_sum)
    recon = own_sum.astype(BF)[None]
    mixed = frozen_sum.astype(F32) + recon_zero + recon_one
    normed = (mixed * mlp_gain).astype(BF)
    mixed_squares = lax.psum(jnp.sum(mixed * mixed, axis=1, keepdims=True), "latent")
    rows = lax.all_gather(normed, "latent", axis=1, tiled=True)
    gate_raw = jnp.dot(rows, w_gate, preferred_element_type=F32)
    up_raw = jnp.dot(rows, w_up, preferred_element_type=F32)
    row_scale = lax.rsqrt(mixed_squares / feats + 1e-06)
    hidden = (jax.nn.gelu(row_scale * gate_raw, approximate=True) * (row_scale * up_raw)).astype(BF)
    partials = jnp.dot(hidden, w_down, preferred_element_type=F32)
    mlp_out = lax.psum_scatter(
        partials, ("layer", "latent"), scatter_dimension=1, tiled=True
    ).astype(BF)
    return (lat_act[None], recon, mlp_out)


def solution(mesh):
    in_specs = (
        P("layer", "token", "latent"),
        P("layer", None),
        P("layer", None, "latent"),
        P("layer", "latent"),
        P("layer", "latent", None),
        P("latent", None),
        P("token", "latent"),
        P("latent"),
        P(None, ("layer", "latent")),
        P(None, ("layer", "latent")),
        P(("layer", "latent"), None),
    )
    out_specs = (
        P("layer", "token", "latent"),
        P("layer", "token", "latent"),
        P("token", ("layer", "latent")),
    )
    small = mesh.shape["layer"] == 2 and mesh.shape["latent"] == 4
    return jax.shard_map(
        blocked if small else general, mesh=mesh, in_specs=in_specs, out_specs=out_specs, check_vma=False
    )
```

```python
import functools

import jax
import jax.numpy as jnp
from jax import lax
from jax.experimental import pallas as pl
from jax.experimental.pallas import tpu as pltpu
from jax.sharding import PartitionSpec as P


BF = jnp.bfloat16
F32 = jnp.float32
VMEM = pl.BlockSpec(memory_space=pltpu.VMEM)
SMEM = pl.BlockSpec(memory_space=pltpu.SMEM)
HBM = pl.BlockSpec(memory_space=pltpu.HBM)
ANY = pl.BlockSpec(memory_space=pl.ANY)
TAIL = 16
PARTS = 2


def dot_cols(x_km, w_kn):
    return lax.dot_general(x_km, w_kn, (((0,), (0,)), ((), ())), preferred_element_type=F32)


def in_block(ids_ref, work):
    pl.when(ids_ref[0] >= 0)(work)


def column_of(row, width):
    n = row.shape[1]
    block = jnp.broadcast_to(row, (128, n)).T
    return jnp.concatenate([block] * (width // 128), axis=1)


def call(kernel, out_shapes, scratch, args, specs, flops, limit, out_specs=None):
    return pl.pallas_call(
        kernel,
        out_shape=out_shapes,
        in_specs=specs,
        out_specs=[VMEM] * len(out_shapes) if out_specs is None else out_specs,
        scratch_shapes=scratch,
        cost_estimate=pl.CostEstimate(flops=2 * flops, transcendentals=0, bytes_accessed=0),
        compiler_params=pltpu.CompilerParams(vmem_limit_bytes=limit << 20),
    )(*args)


def in_hbm(array):
    return pltpu.with_memory_space_constraint(array, pltpu.HBM)


def resident(weights):
    return pltpu.with_memory_space_constraint(weights, pltpu.VMEM)


def pick(total, wanted):
    size = wanted - wanted % 128
    while size > 128 and total % size:
        size -= 128
    return size if total % size == 0 else total


def encode_first(ids, own, other, gain, bias, enc):
    width, tokens = own.shape
    _, lats = enc.shape
    half = 2 * width
    tn = pick(lats, 1024)
    steps = lats // tn
    ahead = 3

    def kernel(
        ids_ref, own_ref, other_ref, gain_ref, bias_ref, enc_ref,
        acc_ref, sq_ref, gain_out, bias_out, rest_ref,
        xg, xown, gbuf, wbuf, sems, small
    ):
        core, side = ids_ref[0], ids_ref[1]
        mine = pl.multiple_of(side * half, half)
        others = pl.multiple_of((1 - side) * half, half)
        loads = [
            pltpu.make_async_copy(own_ref, xown, small.at[0]),
            pltpu.make_async_copy(gain_ref.at[:, pl.ds(mine, half)], gbuf, small.at[1]),
        ]
        later = [
            pltpu.make_async_copy(gain_ref.at[:, pl.ds(others, half)], gain_out, small.at[2]),
            pltpu.make_async_copy(bias_ref, bias_out, small.at[3]),
        ]

        def weights(j):
            cols = pl.ds(j % steps * tn, tn)
            if j < steps:
                return pltpu.make_async_copy(enc_ref.at[pl.ds(mine, half), cols], wbuf.at[:, cols], sems.at[j])
            return pltpu.make_async_copy(enc_ref.at[pl.ds(others, half), cols], rest_ref.at[:, cols], sems.at[j])

        for c in loads:
            c.start()
        for j in range(ahead):
            weights(j).start()
        for c in later:
            c.start()
        for c in loads:
            c.wait()

        def gather():
            xg[pl.ds(pl.multiple_of(core * width, width), width), :] = xown[...]
            xg[pl.ds(pl.multiple_of((1 - core) * width, width), width), :] = other_ref[...]
            values = xg[...].astype(F32)
            squares = jnp.sum(values * values, axis=0, keepdims=True)
            xg[...] = (values * column_of(gbuf[...], tokens)).astype(BF)
            sq_ref[...] = jnp.broadcast_to(squares, sq_ref.shape)

        def apply(j):
            cols = pl.ds(j * tn, tn)
            acc_ref[:, cols] = dot_cols(xg[...], wbuf[:, cols])

        in_block(ids_ref, gather)
        for j in range(2 * steps):
            weights(j).wait()
            if j + ahead < 2 * steps:
                weights(j + ahead).start()
            if j < steps:
                in_block(ids_ref, functools.partial(apply, j))
        for c in later:
            c.wait()

    shape = jax.ShapeDtypeStruct
    outs = [
        shape((tokens, lats), F32),
        shape((8, tokens), F32),
        shape((1, half), F32),
        shape((1, lats), F32),
        shape((half, lats), BF),
    ]
    scratch = [
        pltpu.VMEM((half, tokens), BF),
        pltpu.VMEM((width, tokens), BF),
        pltpu.VMEM((1, half), F32),
        pltpu.VMEM((half, lats), BF),
        pltpu.SemaphoreType.DMA((2 * steps,)),
        pltpu.SemaphoreType.DMA((4,)),
    ]
    specs = [SMEM, HBM, VMEM, HBM, HBM, HBM]
    return call(
        kernel,
        outs,
        scratch,
        (ids, in_hbm(own), other, in_hbm(gain), in_hbm(bias), in_hbm(enc)),
        specs,
        4 * tokens * half * lats,
        16,
    )


def encode_last(ids, own, other, acc, sq, gain, bias, rest, feats, dec, ahead):
    width, tokens = own.shape
    half, lats = rest.shape
    tn = pick(lats, 1024)
    steps = lats // tn

    def kernel(
        ids_ref, own_ref, other_ref, acc_ref, sq_ref, gain_ref, bias_ref, rest_ref, dec_ref,
        lat_ref, out_ref, head_ref, xg, scale, sems
    ):
        core = ids_ref[0]
        load = pltpu.make_async_copy(dec_ref.at[:, pl.ds(0, ahead)], head_ref, sems.at[steps])
        load.start()

        def gather():
            xg[pl.ds(pl.multiple_of(core * width, width), width), :] = own_ref[...]
            xg[pl.ds(pl.multiple_of((1 - core) * width, width), width), :] = other_ref[...]
            values = xg[...].astype(F32)
            squares = jnp.sum(values * values, axis=0, keepdims=True) + sq_ref[0:1, :]
            xg[...] = (values * column_of(gain_ref[...], tokens)).astype(BF)
            scale[...] = jnp.broadcast_to(lax.rsqrt(squares / feats + 1e-06), (128, tokens)).T

        def apply(j):
            cols = pl.ds(j * tn, tn)
            pre = scale[:, 0:1] * (dot_cols(xg[...], rest_ref[:, cols]) + acc_ref[:, cols]) + bias_ref[:, cols]
            lat_ref[:, cols] = jnp.maximum(pre, 0.0).astype(BF)

        in_block(ids_ref, gather)
        writes = []
        for j in range(steps):
            in_block(ids_ref, functools.partial(apply, j))
            cols = pl.ds(j * tn, tn)
            writes.append(pltpu.make_async_copy(lat_ref.at[:, cols], out_ref.at[:, cols], sems.at[j]))
            writes[-1].start()
        for c in writes + [load]:
            c.wait()

    shape = jax.ShapeDtypeStruct((tokens, lats), BF)
    scratch = [pltpu.VMEM((half, tokens), BF), pltpu.VMEM((tokens, 128), F32), pltpu.SemaphoreType.DMA((steps + 1,))]
    args = (ids, own, other, acc, sq, gain, bias, rest, in_hbm(dec))
    specs = [SMEM] + [VMEM] * 7 + [HBM]
    outs = [shape, shape, jax.ShapeDtypeStruct((dec.shape[0], ahead), BF)]
    return call(kernel, outs, scratch, args, specs, 2 * tokens * half * lats, 8, [VMEM, HBM, VMEM])


def decode(ids, lat, head, dec, after, only_first, loads=()):
    tokens, lats = lat.shape
    feats = dec.shape[1]
    start_cols = head.shape[1]
    block = feats // 4
    size = pick(feats - start_cols, 512)
    tails = [(at, size) for at in range(start_cols, feats, size)]
    piece = pick(start_cols, 256)
    rows_of = lats // 2

    def kernel(ids_ref, lat_ref, after_ref, head_ref, dec_ref, *rest):
        load_refs, rest = rest[: len(loads)], rest[len(loads) :]
        snd_ref, oth_ref, own_ref, *rest = rest
        loaded_refs, (wbuf, yt, wsems, sems) = rest[: len(loads)], rest[len(loads) :]
        copies = [
            pltpu.make_async_copy(source.at[:, pl.ds(0, cols)], target, sems.at[i])
            for i, (source, target, (_, cols)) in enumerate(zip(load_refs, loaded_refs, loads))
        ]
        core, side, layer = ids_ref[0], ids_ref[1], ids_ref[2]

        def weights(i):
            at, size = tails[i]
            return [
                pltpu.make_async_copy(
                    dec_ref.at[pl.ds(k * rows_of, rows_of), pl.ds(at, size)],
                    wbuf.at[pl.ds(k * rows_of, rows_of), pl.ds(at - start_cols, size)],
                    wsems.at[i, k],
                )
                for k in range(2)
            ]

        def rows(h, c):
            return pl.ds(pl.multiple_of((2 * h + c) * block, block), block)

        def apply(target, weights_of):
            yt[target, :] = jnp.dot(lat_ref[...], weights_of(), preferred_element_type=F32).T

        def share():
            snd_ref[0] = yt[rows(1 - side, 1 - core), :].astype(BF)
            snd_ref[1] = yt[rows(side, 1 - core), :].astype(BF)
            oth_ref[...] = yt[rows(1 - side, core), :]
            own_ref[...] = yt[rows(side, core), :]

        def work():
            pending = [c for i in range(len(tails)) for c in weights(i)]

            def start(count):
                for _ in range(min(count, len(pending))):
                    pending.pop(0).start()

            start(2)
            for at in range(0, start_cols, piece):
                cols = pl.ds(at, piece)
                in_block(ids_ref, functools.partial(apply, cols, lambda cols=cols: head_ref[:, cols]))
                start(1 if at + piece < start_cols else 0)
            for i, (at, size) in enumerate(tails):
                for c in weights(i):
                    c.wait()
                start(2)
                if i == max(0, len(tails) - 2):
                    start(len(pending))
                    for c in copies:
                        c.start()
                cols = pl.ds(at - start_cols, size)
                in_block(
                    ids_ref, functools.partial(apply, pl.ds(at, size), lambda cols=cols: wbuf[:, cols])
                )
            in_block(ids_ref, share)

        if only_first:
            pl.when(layer == 0)(work)

            @pl.when(layer != 0)
            def _():
                for c in copies:
                    c.start()
        else:
            work()
        for c in copies:
            c.wait()

    shape = jax.ShapeDtypeStruct
    outs = [shape((2, block, tokens), BF), shape((block, tokens), F32), shape((block, tokens), F32)]
    outs += [shape((v.shape[0], cols), v.dtype) for v, cols in loads]
    scratch = [
        pltpu.VMEM((lats, feats - start_cols), BF),
        pltpu.VMEM((feats, tokens), F32),
        pltpu.SemaphoreType.DMA((len(tails), 2)),
        pltpu.SemaphoreType.DMA((max(1, len(loads)),)),
    ]
    args = (ids, lat, after, head, in_hbm(dec)) + tuple(in_hbm(v) for v, _ in loads)
    specs = [SMEM, VMEM, ANY, VMEM, HBM] + [HBM] * len(loads)
    return call(kernel, outs, scratch, args, specs, 2 * tokens * lats * feats, 20)


def part_of(rows, i):
    return pl.ds(i * (rows // PARTS), rows // PARTS)


def send_sum(oth, got):
    rows, tokens = oth.shape

    def kernel(oth_ref, got_ref, *out_refs):
        for i, out_ref in enumerate(out_refs):
            at = part_of(rows, i)
            out_ref[...] = (oth_ref[at, :] + got_ref[0, at, :].astype(F32)).astype(BF)

    outs = [jax.ShapeDtypeStruct((rows // PARTS, tokens), BF)] * PARTS
    return call(kernel, outs, [], (oth, got), [VMEM] * 2, oth.size, 4)


def next_send(oth, got):
    def kernel(oth_ref, got_ref, out_ref):
        out_ref[...] = (oth_ref[...] + got_ref[0].astype(F32)).astype(BF)

    return call(kernel, [jax.ShapeDtypeStruct(oth.shape, BF)], [], (oth, got), [VMEM] * 2, oth.size, 4)[0]


def layer_sum(ids, i, own, got, back, q_own, q_got, q_back):
    rows, tokens = own.shape
    at = part_of(rows, i)

    def kernel(ids_ref, own_ref, got_ref, back_ref, qo_ref, qg_ref, qb_ref, sum_ref, out_ref):
        total = own_ref[at, :] + got_ref[1, at, :].astype(F32) + back_ref[...].astype(F32)
        sum_ref[...] = total

        @pl.when(ids_ref[2] == 0)
        def _():
            extra = qo_ref[at, :] + qg_ref[1, at, :].astype(F32) + qb_ref[at, :].astype(F32)
            sum_ref[...] = sum_ref[...] + extra

        out_ref[...] = sum_ref[...].astype(BF)

    shape = jax.ShapeDtypeStruct
    outs = [shape((rows // PARTS, tokens), F32), shape((rows // PARTS, tokens), BF)]
    args = (ids, own, got, back, q_own, q_got, q_back)
    return call(kernel, outs, [], args, [SMEM] + [VMEM] * 6, own.size, 5)


def next_sum(own, got, back):
    def kernel(own_ref, got_ref, back_ref, out_ref):
        out_ref[...] = (own_ref[...] + got_ref[1].astype(F32) + back_ref[...].astype(F32)).astype(BF)

    outs = [jax.ShapeDtypeStruct(own.shape, BF)]
    return call(kernel, outs, [], (own, got, back), [VMEM] * 3, own.size, 4)[0]


def recon_sum(own, got, extra, backs):
    rows, _ = own.shape

    def kernel(own_ref, got_ref, extra_ref, *refs):
        *back_refs, out_ref = refs
        for i, back_ref in enumerate(back_refs):
            at = part_of(rows, i)
            total = own_ref[at, :] + got_ref[1, at, :].astype(F32) + back_ref[...].astype(F32)
            out_ref[at, :] = (total + extra_ref[at, :].astype(F32)).astype(BF)

    outs = [jax.ShapeDtypeStruct(own.shape, BF)]
    return call(kernel, outs, [], (own, got, extra) + tuple(backs), [VMEM] * (3 + len(backs)), own.size, 5)[0]


def mix(i, target, other, frozen, gain):
    part, tokens = target.shape
    at = pl.ds(i * part, part)

    def kernel(t_ref, o_ref, f_ref, g_ref, out_ref):
        mixed = f_ref[at, :].astype(F32) + t_ref[...] + o_ref[...].astype(F32)
        gains = column_of(g_ref[...][None, :], tokens)
        out_ref[pl.ds(0, part), :] = (mixed * gains[i * part : (i + 1) * part, :]).astype(BF)
        squares = jnp.sum(mixed * mixed, axis=0, keepdims=True)
        high = squares.astype(BF).astype(F32)
        rest = squares - high
        mid = rest.astype(BF).astype(F32)
        low = rest - mid
        row = lax.broadcasted_iota(jnp.int32, (TAIL, tokens), 0)
        tail = jnp.where(row == 0, high, jnp.where(row == 1, mid, jnp.where(row == 2, low, 0.0)))
        out_ref[pl.ds(part, TAIL), :] = tail.astype(BF)

    outs = [jax.ShapeDtypeStruct((part + TAIL, tokens), BF)]
    return call(kernel, outs, [], (target, other, frozen, gain), [VMEM] * 4, part * tokens, 5)[0]


def fold(keep, got):
    count, piece, tokens = keep.shape

    def kernel(keep_ref, got_ref, own_ref, *sent):
        own_ref[...] = keep_ref[0] + got_ref[0].astype(F32)
        for i in range(1, count):
            sent[i - 1][...] = (keep_ref[i] + got_ref[i].astype(F32)).astype(BF)

    shape = jax.ShapeDtypeStruct
    outs = [shape((piece, tokens), F32)] + [shape((piece, tokens), BF)] * (count - 1)
    return call(kernel, outs, [], (keep, got), [VMEM] * 2, count * piece * tokens, 6)


def last_sum(own, *others):
    def kernel(own_ref, *refs):
        *other_refs, out_ref = refs
        total = own_ref[...]
        for r in other_refs:
            total = total + r[...].astype(F32)
        out_ref[...] = total.astype(BF)

    outs = [jax.ShapeDtypeStruct(own.shape, BF)]
    return call(kernel, outs, [], (own,) + others, [VMEM] * (1 + len(others)), own.size, 4)[0]


def mlp_half(ids, owns, others, w_gate, w_up, first, extra, layers):
    part, tokens = owns[0].shape[0] - TAIL, owns[0].shape[1]
    width = part * PARTS
    half = 2 * width
    feats, units = w_gate.shape
    piece = feats // (4 * layers)
    tn = pick(feats, 768)

    def kernel(ids_ref, *rest):
        own_refs, other_refs, (wg_ref, wu_ref, *rest) = rest[:PARTS], rest[PARTS : 2 * PARTS], rest[2 * PARTS :]
        if first:
            g_ref, u_ref, sq_ref, xg = rest
        else:
            g_in, u_in, sq_in, wd_ref, snd_ref, keep_ref, xg, yt = rest
        core, side = ids_ref[0], ids_ref[1]
        row = side if first else 1 - side
        row = pl.multiple_of(row * half, half)
        squares = jnp.zeros((1, tokens), F32)
        for refs, c in ((own_refs, core), (other_refs, 1 - core)):
            for i, ref in enumerate(refs):
                xg[pl.ds(pl.multiple_of(c * width + i * part, part), part), :] = ref[pl.ds(0, part), :]
                squares += jnp.sum(ref[pl.ds(part, TAIL), :].astype(F32), axis=0, keepdims=True)
        gate = dot_cols(xg[...], wg_ref[pl.ds(row, half), :])
        up = dot_cols(xg[...], wu_ref[pl.ds(row, half), :])
        if first:
            g_ref[...] = gate
            u_ref[...] = up
            sq_ref[...] = jnp.broadcast_to(squares, sq_ref.shape)
            return
        total = squares + sq_in[0:1, :]
        scale = jnp.broadcast_to(lax.rsqrt(total / feats + 1e-06), (128, tokens)).T[:, 0:1]
        gate = scale * (gate + g_in[...])
        up = scale * (up + u_in[...])
        hidden = (jax.nn.gelu(gate, approximate=True) * up).astype(BF)
        for n in range(feats // tn):
            cols = pl.ds(n * tn, tn)
            yt[cols, :] = jnp.dot(hidden, wd_ref[:, cols], preferred_element_type=F32).T
        layer = ids_ref[2]
        for i in range(4):
            at = ((layer ^ (i >> 1)) * 2 + (side ^ (i & 1))) * 2
            snd_ref[i] = yt[pl.ds(pl.multiple_of((at + 1 - core) * piece, piece), piece), :].astype(BF)
            keep_ref[i] = yt[pl.ds(pl.multiple_of((at + core) * piece, piece), piece), :]

    shape = jax.ShapeDtypeStruct
    scratch = [pltpu.VMEM((half, tokens), BF)]
    if first:
        outs = [shape((tokens, units), F32), shape((tokens, units), F32), shape((8, tokens), F32)]
    else:
        outs = [shape((4, piece, tokens), BF), shape((4, piece, tokens), F32)]
        scratch += [pltpu.VMEM((feats, tokens), F32)]
    args = (ids, *owns, *others, w_gate, w_up) + extra
    flops = 4 * tokens * half * units + (0 if first else 2 * tokens * units * feats)
    return call(kernel, outs, scratch, args, [SMEM] + [VMEM] * (len(args) - 1), flops, 6 if first else 12)


def blocked(
    resid_in, clt_gain, enc_w, enc_b, dec_same, dec_next, frozen_sum, mlp_gain, w_gate, w_up, w_down
):
    return blocked_steps(
        resid_in, clt_gain, enc_w, enc_b, dec_same, dec_next, frozen_sum, mlp_gain, w_gate, w_up, w_down
    )


def blocked_steps(
    resid_in, clt_gain, enc_w, enc_b, dec_same, dec_next, frozen_sum, mlp_gain, w_gate, w_up, w_down
):
    layers = lax.axis_size("layer")
    both = ("layer", "latent")
    place = lax.axis_index("latent")
    layer = lax.axis_index("layer")
    ids = jnp.stack([place & 1, place >> 1, layer]).astype(jnp.int32)

    def partner(v):
        return lax.ppermute(v, "latent", [(i, i ^ 1) for i in range(4)])

    def across(v):
        return lax.ppermute(v, "latent", [(i, i ^ 2) for i in range(4)])

    def other_layer(v):
        return lax.ppermute(v, "layer", [(0, 1), (1, 0)])

    own = resid_in[0].T
    far = across(own)
    near = partner(own)
    parts = encode_first(ids, own, near, clt_gain, enc_b, enc_w[0])
    far_near = partner(far)
    ahead = pick(dec_next.shape[1], 768)
    lat, lat_out, head = encode_last(ids, far, far_near, *parts, enc_w.shape[1], dec_next, ahead)

    def to_partner(snd, pairs):
        return lax.ppermute(snd, both, [(i, i ^ 1) for i in pairs])

    def to_chip(sent, pairs):
        return lax.ppermute(sent, both, [(i, i ^ 2) for i in pairs])

    same, frozen = dec_same[0], frozen_sum.T
    first, every = range(4), range(8)
    snd, oth, q_own, head = decode(ids, lat, head, dec_next, lat, True, ((same, ahead),))
    q_got = to_partner(snd, first)
    q_sent = next_send(oth, q_got)
    q_back = to_chip(q_sent, first)
    snd, oth, own, frozen = decode(ids, lat, head, same, snd, False, ((frozen, frozen.shape[1]),))
    got = to_partner(snd, every)
    sents = send_sum(oth, got)
    backs = [to_chip(sent, every) for sent in sents]
    normed = []
    for i, back in enumerate(backs):
        total, sent = layer_sum(ids, i, own, got, back, q_own, q_got, q_back)
        normed.append(mix(i, total, other_layer(sent), frozen, mlp_gain))
    w_gate, w_up, w_down = resident(w_gate), resident(w_up), resident(w_down)
    n_near = [partner(v) for v in normed]
    n_far = [across(v) for v in normed]
    q_here = lax.ppermute(next_sum(q_own, q_got, q_back), "layer", [(0, 1)])
    recon = recon_sum(own, got, q_here, backs)
    g, u, nsq = mlp_half(ids, normed, n_near, w_gate, w_up, True, (), layers)
    n_far_near = [partner(v) for v in n_far]
    snd, keep = mlp_half(ids, n_far, n_far_near, w_gate, w_up, False, (g, u, nsq, w_down), layers)
    got = partner(snd)
    kept, to_y, to_x, to_d = fold(keep, got)
    r_d = lax.ppermute(to_d, both, [(i, i ^ 6) for i in range(8)])
    r_x = other_layer(to_x)
    r_y = across(to_y)
    out = last_sum(kept, r_x, r_y, r_d)
    return (lat_out[None], recon.T[None], out.T)


def passed_along(block, axis, distance):
    devices = range(lax.axis_size(axis))
    route = [(i - distance, i) for i in devices if i - distance in devices]
    return lax.ppermute(block, axis, route)


def swapped_with(value, axis, stride):
    mask = 2**stride
    pairs = [(source, source ^ mask) for source in range(lax.axis_size(axis))]
    return lax.ppermute(value, axis, pairs)


def general(
    resid_in, clt_gain, enc_w, enc_b, dec_same, dec_next, frozen_sum, mlp_gain, w_gate, w_up, w_down
):
    own_rows = resid_in[0]
    feats = enc_w.shape[1]
    own_values = own_rows.astype(F32)
    squares = lax.psum(jnp.sum(own_values * own_values, axis=1, keepdims=True), "latent")
    gated = (lax.all_gather(own_rows, "latent", axis=1, tiled=True).astype(F32) * clt_gain[0]).astype(BF)
    projected = jnp.dot(gated, enc_w[0], preferred_element_type=F32)
    inv_scale = lax.rsqrt(squares / feats + 1e-06)
    lat_act = jnp.maximum(inv_scale * projected + enc_b[0], 0.0).astype(BF)
    is_first = lax.axis_index("layer") == 0
    own_term = jnp.dot(lat_act, dec_same[0], preferred_element_type=F32)
    arrived = passed_along(lat_act, "layer", 1)
    target_term = own_term + jnp.dot(arrived, dec_next, preferred_element_type=F32)
    own_sum = lax.psum_scatter(target_term, "latent", scatter_dimension=1, tiled=True)
    other_sum = swapped_with(own_sum, "layer", 0)
    recon_zero = jnp.where(is_first, own_sum, other_sum)
    recon_one = jnp.where(is_first, other_sum, own_sum)
    recon = own_sum.astype(BF)[None]
    mixed = frozen_sum.astype(F32) + recon_zero + recon_one
    normed = (mixed * mlp_gain).astype(BF)
    mixed_squares = lax.psum(jnp.sum(mixed * mixed, axis=1, keepdims=True), "latent")
    rows = lax.all_gather(normed, "latent", axis=1, tiled=True)
    gate_raw = jnp.dot(rows, w_gate, preferred_element_type=F32)
    up_raw = jnp.dot(rows, w_up, preferred_element_type=F32)
    row_scale = lax.rsqrt(mixed_squares / feats + 1e-06)
    hidden = (jax.nn.gelu(row_scale * gate_raw, approximate=True) * (row_scale * up_raw)).astype(BF)
    partials = jnp.dot(hidden, w_down, preferred_element_type=F32)
    mlp_out = lax.psum_scatter(
        partials, ("layer", "latent"), scatter_dimension=1, tiled=True
    ).astype(BF)
    return (lat_act[None], recon, mlp_out)


def solution(mesh):
    in_specs = (
        P("layer", "token", "latent"),
        P("layer", None),
        P("layer", None, "latent"),
        P("layer", "latent"),
        P("layer", "latent", None),
        P("latent", None),
        P("token", "latent"),
        P("latent"),
        P(None, ("layer", "latent")),
        P(None, ("layer", "latent")),
        P(("layer", "latent"), None),
    )
    out_specs = (
        P("layer", "token", "latent"),
        P("layer", "token", "latent"),
        P("token", ("layer", "latent")),
    )
    small = mesh.shape["layer"] == 2 and mesh.shape["latent"] == 4
    return jax.shard_map(
        blocked if small else general, mesh=mesh, in_specs=in_specs, out_specs=out_specs, check_vma=False
    )
```

```python
import functools

import jax
import jax.numpy as jnp
from jax import lax
from jax.experimental import pallas as pl
from jax.experimental.pallas import tpu as pltpu
from jax.sharding import PartitionSpec as P


BF = jnp.bfloat16
F32 = jnp.float32
VMEM = pl.BlockSpec(memory_space=pltpu.VMEM)
HBM = pl.BlockSpec(memory_space=pltpu.HBM)
ANY = pl.BlockSpec(memory_space=pl.ANY)
TAIL = 16
PARTS = 2
TRANSFER = 4 << 30


def dot_cols(x_km, w_kn):
    return lax.dot_general(x_km, w_kn, (((0,), (0,)), ((), ())), preferred_element_type=F32)


def whereabouts():
    place = lax.axis_index("latent")
    return place & 1, place >> 1, lax.axis_index("layer")


def in_block(work):
    pl.when(lax.axis_index("latent") >= 0)(work)


def column_of(row, width):
    n = row.shape[1]
    block = jnp.broadcast_to(row, (128, n)).T
    return jnp.concatenate([block] * (width // 128), axis=1)


def call(kernel, out_shapes, scratch, args, specs, flops, limit, out_specs=None):
    return pl.pallas_call(
        kernel,
        out_shape=out_shapes,
        in_specs=specs,
        out_specs=[VMEM] * len(out_shapes) if out_specs is None else out_specs,
        scratch_shapes=scratch,
        cost_estimate=pl.CostEstimate(flops=flops, transcendentals=0, bytes_accessed=0),
        compiler_params=pltpu.CompilerParams(vmem_limit_bytes=limit << 20),
    )(*args)


def in_hbm(array):
    return pltpu.with_memory_space_constraint(array, pltpu.HBM)


def resident(weights):
    return pltpu.with_memory_space_constraint(weights, pltpu.VMEM)


def pick(total, wanted):
    size = wanted - wanted % 128
    while size > 128 and total % size:
        size -= 128
    return size if total % size == 0 else total


def encode_first(own, other, gain, bias, enc):
    width, tokens = own.shape
    _, lats = enc.shape
    half = 2 * width
    tn = pick(lats, 1024)
    steps = lats // tn
    ahead = 3

    def kernel(
        own_ref, other_ref, gain_ref, bias_ref, enc_ref,
        acc_ref, sq_ref, gain_out, bias_out, rest_ref,
        xg, xown, gbuf, wbuf, sems, small
    ):
        core, side, _ = whereabouts()
        mine = pl.multiple_of(side * half, half)
        others = pl.multiple_of((1 - side) * half, half)
        loads = [
            pltpu.make_async_copy(own_ref, xown, small.at[0]),
            pltpu.make_async_copy(gain_ref.at[:, pl.ds(mine, half)], gbuf, small.at[1]),
        ]
        later = [
            pltpu.make_async_copy(gain_ref.at[:, pl.ds(others, half)], gain_out, small.at[2]),
            pltpu.make_async_copy(bias_ref, bias_out, small.at[3]),
        ]

        def weights(j):
            cols = pl.ds(j % steps * tn, tn)
            if j < steps:
                return pltpu.make_async_copy(enc_ref.at[pl.ds(mine, half), cols], wbuf.at[:, cols], sems.at[j])
            return pltpu.make_async_copy(enc_ref.at[pl.ds(others, half), cols], rest_ref.at[:, cols], sems.at[j])

        for c in loads:
            c.start()
        for j in range(ahead):
            weights(j).start()
        for c in later:
            c.start()
        for c in loads:
            c.wait()

        def gather():
            xg[pl.ds(pl.multiple_of(core * width, width), width), :] = xown[...]
            xg[pl.ds(pl.multiple_of((1 - core) * width, width), width), :] = other_ref[...]
            values = xg[...].astype(F32)
            squares = jnp.sum(values * values, axis=0, keepdims=True)
            xg[...] = (values * column_of(gbuf[...], tokens)).astype(BF)
            sq_ref[...] = jnp.broadcast_to(squares, sq_ref.shape)

        def apply(j):
            cols = pl.ds(j * tn, tn)
            acc_ref[:, cols] = dot_cols(xg[...], wbuf[:, cols])

        in_block(gather)
        for j in range(2 * steps):
            weights(j).wait()
            if j + ahead < 2 * steps:
                weights(j + ahead).start()
            if j < steps:
                in_block(functools.partial(apply, j))
        for c in later:
            c.wait()

    shape = jax.ShapeDtypeStruct
    outs = [
        shape((tokens, lats), F32),
        shape((8, tokens), F32),
        shape((1, half), F32),
        shape((1, lats), F32),
        shape((half, lats), BF),
    ]
    scratch = [
        pltpu.VMEM((half, tokens), BF),
        pltpu.VMEM((width, tokens), BF),
        pltpu.VMEM((1, half), F32),
        pltpu.VMEM((half, lats), BF),
        pltpu.SemaphoreType.DMA((2 * steps,)),
        pltpu.SemaphoreType.DMA((4,)),
    ]
    specs = [HBM, VMEM, HBM, HBM, HBM]
    return call(
        kernel,
        outs,
        scratch,
        (in_hbm(own), other, in_hbm(gain), in_hbm(bias), in_hbm(enc)),
        specs,
        8 * tokens * half * lats,
        16,
    )


def encode_last(own, other, acc, sq, gain, bias, rest, feats, dec, ahead):
    width, tokens = own.shape
    half, lats = rest.shape
    tn = pick(lats, 1024)
    steps = lats // tn

    def kernel(
        own_ref, other_ref, acc_ref, sq_ref, gain_ref, bias_ref, rest_ref, dec_ref,
        lat_ref, head_ref, xg, scale, sems
    ):
        core = whereabouts()[0]
        load = pltpu.make_async_copy(dec_ref.at[:, pl.ds(0, ahead)], head_ref, sems.at[0])
        load.start()

        def gather():
            xg[pl.ds(pl.multiple_of(core * width, width), width), :] = own_ref[...]
            xg[pl.ds(pl.multiple_of((1 - core) * width, width), width), :] = other_ref[...]
            values = xg[...].astype(F32)
            squares = jnp.sum(values * values, axis=0, keepdims=True) + sq_ref[0:1, :]
            xg[...] = (values * column_of(gain_ref[...], tokens)).astype(BF)
            scale[...] = jnp.broadcast_to(lax.rsqrt(squares / feats + 1e-06), (128, tokens)).T

        def apply(j):
            cols = pl.ds(j * tn, tn)
            pre = scale[:, 0:1] * (dot_cols(xg[...], rest_ref[:, cols]) + acc_ref[:, cols]) + bias_ref[:, cols]
            lat_ref[:, cols] = jnp.maximum(pre, 0.0).astype(BF)

        def work():
            gather()
            for j in range(steps):
                apply(j)

        in_block(work)
        load.wait()

    shape = jax.ShapeDtypeStruct((tokens, lats), BF)
    scratch = [pltpu.VMEM((half, tokens), BF), pltpu.VMEM((tokens, 128), F32), pltpu.SemaphoreType.DMA((1,))]
    args = (own, other, acc, sq, gain, bias, rest, in_hbm(dec))
    specs = [VMEM] * 7 + [HBM]
    outs = [shape, jax.ShapeDtypeStruct((dec.shape[0], ahead), BF)]
    return call(kernel, outs, scratch, args, specs, 2 * tokens * half * lats, 8)


def decode_head(lat, head, dec, after, more):
    tokens, lats = lat.shape
    cols = head.shape[1]

    def kernel(lat_ref, after_ref, head_ref, dec_ref, yt_ref, more_ref, sems):
        load = pltpu.make_async_copy(dec_ref.at[:, pl.ds(cols, more)], more_ref, sems.at[0])
        load.start()

        def work():
            yt_ref[...] = jnp.dot(lat_ref[...], head_ref[...], preferred_element_type=F32).T

        in_block(work)
        load.wait()

    outs = [jax.ShapeDtypeStruct((cols, tokens), F32), jax.ShapeDtypeStruct((lats, more), BF)]
    args = (lat, after, head, in_hbm(dec))
    return call(
        kernel, outs, [pltpu.SemaphoreType.DMA((1,))], args, [VMEM, ANY, VMEM, HBM],
        2 * tokens * lats * cols, 5,
    )


def decode(lat, done, head, dec, after, only_first, loads=(), write=False):
    tokens, lats = lat.shape
    feats = dec.shape[1]
    ready = 0 if done is None else done.shape[0]
    loaded = ready + head.shape[1]
    block = feats // 4
    size = pick(feats - loaded, 512)
    tails = [(at, size) for at in range(loaded, feats, size)]
    piece = pick(loaded - ready, 256)
    rows_of = lats // 2

    def kernel(lat_ref, after_ref, head_ref, dec_ref, *rest):
        if ready:
            done_ref, *rest = rest
        load_refs, rest = rest[: len(loads)], rest[len(loads) :]
        snd_ref, oth_ref, own_ref, *rest = rest
        loaded_refs, rest = rest[: len(loads)], rest[len(loads) :]
        if write:
            lat_out, *rest = rest
        wbuf, yt, wsems, sems = rest
        copies = [
            pltpu.make_async_copy(source.at[:, pl.ds(0, cols)], target, sems.at[i])
            for i, (source, target, (_, cols)) in enumerate(zip(load_refs, loaded_refs, loads))
        ]
        if write:
            copies.append(pltpu.make_async_copy(lat_ref, lat_out, sems.at[len(loads)]))
        core, side, layer = whereabouts()

        def weights(i):
            at, size = tails[i]
            return [
                pltpu.make_async_copy(
                    dec_ref.at[pl.ds(k * rows_of, rows_of), pl.ds(at, size)],
                    wbuf.at[pl.ds(k * rows_of, rows_of), pl.ds(at - loaded, size)],
                    wsems.at[i, k],
                )
                for k in range(2)
            ]

        def rows(h, c):
            return pl.ds(pl.multiple_of((2 * h + c) * block, block), block)

        def apply(target, weights_of):
            yt[target, :] = jnp.dot(lat_ref[...], weights_of(), preferred_element_type=F32).T

        def share():
            snd_ref[0] = yt[rows(1 - side, 1 - core), :].astype(BF)
            snd_ref[1] = yt[rows(side, 1 - core), :].astype(BF)
            oth_ref[...] = yt[rows(1 - side, core), :]
            own_ref[...] = yt[rows(side, core), :]

        def bring():
            yt[pl.ds(0, ready), :] = done_ref[...]

        def work():
            pending = [c for i in range(len(tails)) for c in weights(i)]

            def start(count):
                for _ in range(min(count, len(pending))):
                    pending.pop(0).start()

            start(2)
            if ready:
                in_block(bring)
            for at in range(0, loaded - ready, piece):
                cols = pl.ds(at, piece)
                target = pl.ds(ready + at, piece)
                in_block(functools.partial(apply, target, lambda cols=cols: head_ref[:, cols]))
                start(1 if at + piece < loaded - ready else 0)
            for i, (at, size) in enumerate(tails):
                for c in weights(i):
                    c.wait()
                start(2)
                if i == max(0, len(tails) - 2):
                    start(len(pending))
                    for c in copies:
                        c.start()
                cols = pl.ds(at - loaded, size)
                in_block(
                    functools.partial(apply, pl.ds(at, size), lambda cols=cols: wbuf[:, cols])
                )
            in_block(share)

        if only_first:
            pl.when(layer == 0)(work)

            @pl.when(layer != 0)
            def _():
                for c in copies:
                    c.start()
        else:
            work()
        for c in copies:
            c.wait()

    shape = jax.ShapeDtypeStruct
    outs = [shape((2, block, tokens), BF), shape((block, tokens), F32), shape((block, tokens), F32)]
    outs += [shape((v.shape[0], cols), v.dtype) for v, cols in loads]
    out_specs = [VMEM] * len(outs)
    if write:
        outs, out_specs = outs + [shape(lat.shape, lat.dtype)], out_specs + [HBM]
    scratch = [
        pltpu.VMEM((lats, feats - loaded), BF),
        pltpu.VMEM((feats, tokens), F32),
        pltpu.SemaphoreType.DMA((len(tails), 2)),
        pltpu.SemaphoreType.DMA((len(loads) + 1,)),
    ]
    args = (lat, after, head, in_hbm(dec)) + ((done,) if ready else ()) + tuple(in_hbm(v) for v, _ in loads)
    specs = [VMEM, ANY, VMEM, HBM] + [VMEM] * (ready > 0) + [HBM] * len(loads)
    limit = 8 + lats * (feats - loaded) * 2 // (1 << 20)
    return call(kernel, outs, scratch, args, specs, 2 * tokens * lats * (feats - ready), limit, out_specs)


def part_of(rows, i):
    return pl.ds(i * (rows // PARTS), rows // PARTS)


def send_sum(oth, got):
    rows, tokens = oth.shape

    def kernel(oth_ref, got_ref, *out_refs):
        for i, out_ref in enumerate(out_refs):
            at = part_of(rows, i)
            out_ref[...] = (oth_ref[at, :] + got_ref[0, at, :].astype(F32)).astype(BF)

    outs = [jax.ShapeDtypeStruct((rows // PARTS, tokens), BF)] * PARTS
    return call(kernel, outs, [], (oth, got), [VMEM] * 2, TRANSFER, 4)


def next_send(oth, got):
    def kernel(oth_ref, got_ref, out_ref):
        out_ref[...] = (oth_ref[...] + got_ref[0].astype(F32)).astype(BF)

    return call(kernel, [jax.ShapeDtypeStruct(oth.shape, BF)], [], (oth, got), [VMEM] * 2, oth.size, 4)[0]


def layer_sum(i, own, got, back, q_own, q_got, q_back):
    rows, tokens = own.shape
    at = part_of(rows, i)

    def kernel(own_ref, got_ref, back_ref, qo_ref, qg_ref, qb_ref, sum_ref, out_ref):
        total = own_ref[at, :] + got_ref[1, at, :].astype(F32) + back_ref[...].astype(F32)
        sum_ref[...] = total

        @pl.when(whereabouts()[2] == 0)
        def _():
            extra = qo_ref[at, :] + qg_ref[1, at, :].astype(F32) + qb_ref[at, :].astype(F32)
            sum_ref[...] = sum_ref[...] + extra

        out_ref[...] = sum_ref[...].astype(BF)

    shape = jax.ShapeDtypeStruct
    outs = [shape((rows // PARTS, tokens), F32), shape((rows // PARTS, tokens), BF)]
    args = (own, got, back, q_own, q_got, q_back)
    return call(kernel, outs, [], args, [VMEM] * 6, TRANSFER, 5)


def next_sum(own, got, back):
    def kernel(own_ref, got_ref, back_ref, out_ref):
        out_ref[...] = (own_ref[...] + got_ref[1].astype(F32) + back_ref[...].astype(F32)).astype(BF)

    outs = [jax.ShapeDtypeStruct(own.shape, BF)]
    return call(kernel, outs, [], (own, got, back), [VMEM] * 3, own.size, 4)[0]


def recon_sum(own, got, extra, backs):
    rows, _ = own.shape

    def kernel(own_ref, got_ref, extra_ref, *refs):
        *back_refs, out_ref = refs
        from_first = whereabouts()[2] == 1
        for i, back_ref in enumerate(back_refs):
            at = part_of(rows, i)
            total = own_ref[at, :] + got_ref[1, at, :].astype(F32) + back_ref[...].astype(F32)
            extra = jnp.where(from_first, extra_ref[at, :].astype(F32), 0.0)
            out_ref[at, :] = (total + extra).astype(BF)

    outs = [jax.ShapeDtypeStruct(own.shape, BF)]
    args = (own, got, extra) + tuple(backs)
    return call(kernel, outs, [], args, [VMEM] * (3 + len(backs)), own.size, 5)[0]


def mix(i, target, other, frozen, gain):
    part, tokens = target.shape
    at = pl.ds(i * part, part)

    def kernel(t_ref, o_ref, f_ref, g_ref, out_ref):
        mixed = f_ref[at, :].astype(F32) + t_ref[...] + o_ref[...].astype(F32)
        gains = column_of(g_ref[...][None, :], tokens)
        out_ref[pl.ds(0, part), :] = (mixed * gains[i * part : (i + 1) * part, :]).astype(BF)
        squares = jnp.sum(mixed * mixed, axis=0, keepdims=True)
        high = squares.astype(BF).astype(F32)
        rest = squares - high
        mid = rest.astype(BF).astype(F32)
        low = rest - mid
        row = lax.broadcasted_iota(jnp.int32, (TAIL, tokens), 0)
        tail = jnp.where(row == 0, high, jnp.where(row == 1, mid, jnp.where(row == 2, low, 0.0)))
        out_ref[pl.ds(part, TAIL), :] = tail.astype(BF)

    outs = [jax.ShapeDtypeStruct((part + TAIL, tokens), BF)]
    return call(kernel, outs, [], (target, other, frozen, gain), [VMEM] * 4, TRANSFER, 5)[0]


def fold(keep, got):
    count, piece, tokens = keep.shape

    def kernel(keep_ref, got_ref, own_ref, *sent):
        own_ref[...] = keep_ref[0] + got_ref[0].astype(F32)
        for i in range(1, count):
            sent[i - 1][...] = (keep_ref[i] + got_ref[i].astype(F32)).astype(BF)

    shape = jax.ShapeDtypeStruct
    outs = [shape((piece, tokens), F32)] + [shape((piece, tokens), BF)] * (count - 1)
    return call(kernel, outs, [], (keep, got), [VMEM] * 2, count * piece * tokens, 6)


def last_sum(own, *others):
    def kernel(own_ref, *refs):
        *other_refs, out_ref = refs
        total = own_ref[...]
        for r in other_refs:
            total = total + r[...].astype(F32)
        out_ref[...] = total.astype(BF)

    outs = [jax.ShapeDtypeStruct(own.shape, BF)]
    return call(kernel, outs, [], (own,) + others, [VMEM] * (1 + len(others)), own.size, 4)[0]


def mlp_half(owns, others, w_gate, w_up, first, extra, layers):
    part, tokens = owns[0].shape[0] - TAIL, owns[0].shape[1]
    width = part * PARTS
    half = 2 * width
    feats, units = w_gate.shape
    piece = feats // (4 * layers)
    tn = pick(feats, 768)

    def kernel(*rest):
        own_refs, other_refs, (wg_ref, wu_ref, *rest) = rest[:PARTS], rest[PARTS : 2 * PARTS], rest[2 * PARTS :]
        if first:
            g_ref, u_ref, sq_ref, xg = rest
        else:
            g_in, u_in, sq_in, wd_ref, snd_ref, keep_ref, xg, yt = rest
        core, side, layer = whereabouts()
        row = side if first else 1 - side
        row = pl.multiple_of(row * half, half)
        squares = jnp.zeros((1, tokens), F32)
        for refs, c in ((own_refs, core), (other_refs, 1 - core)):
            for i, ref in enumerate(refs):
                xg[pl.ds(pl.multiple_of(c * width + i * part, part), part), :] = ref[pl.ds(0, part), :]
                squares += jnp.sum(ref[pl.ds(part, TAIL), :].astype(F32), axis=0, keepdims=True)
        gate = dot_cols(xg[...], wg_ref[pl.ds(row, half), :])
        up = dot_cols(xg[...], wu_ref[pl.ds(row, half), :])
        if first:
            g_ref[...] = gate
            u_ref[...] = up
            sq_ref[...] = jnp.broadcast_to(squares, sq_ref.shape)
            return
        total = squares + sq_in[0:1, :]
        scale = jnp.broadcast_to(lax.rsqrt(total / feats + 1e-06), (128, tokens)).T[:, 0:1]
        gate = scale * (gate + g_in[...])
        up = scale * (up + u_in[...])
        hidden = (jax.nn.gelu(gate, approximate=True) * up).astype(BF)
        for n in range(feats // tn):
            cols = pl.ds(n * tn, tn)
            yt[cols, :] = jnp.dot(hidden, wd_ref[:, cols], preferred_element_type=F32).T
        for i in range(4):
            at = ((layer ^ (i >> 1)) * 2 + (side ^ (i & 1))) * 2
            snd_ref[i] = yt[pl.ds(pl.multiple_of((at + 1 - core) * piece, piece), piece), :].astype(BF)
            keep_ref[i] = yt[pl.ds(pl.multiple_of((at + core) * piece, piece), piece), :]

    shape = jax.ShapeDtypeStruct
    scratch = [pltpu.VMEM((half, tokens), BF)]
    if first:
        outs = [shape((tokens, units), F32), shape((tokens, units), F32), shape((8, tokens), F32)]
    else:
        outs = [shape((4, piece, tokens), BF), shape((4, piece, tokens), F32)]
        scratch += [pltpu.VMEM((feats, tokens), F32)]
    args = (*owns, *others, w_gate, w_up) + extra
    flops = 4 * tokens * half * units + (0 if first else 2 * tokens * units * feats)
    return call(kernel, outs, scratch, args, [VMEM] * len(args), flops, 6 if first else 12)


def blocked(
    resid_in, clt_gain, enc_w, enc_b, dec_same, dec_next, frozen_sum, mlp_gain, w_gate, w_up, w_down
):
    return blocked_steps(
        resid_in, clt_gain, enc_w, enc_b, dec_same, dec_next, frozen_sum, mlp_gain, w_gate, w_up, w_down
    )


def blocked_steps(
    resid_in, clt_gain, enc_w, enc_b, dec_same, dec_next, frozen_sum, mlp_gain, w_gate, w_up, w_down
):
    layers = lax.axis_size("layer")
    both = ("layer", "latent")

    def partner(v):
        return lax.ppermute(v, "latent", [(i, i ^ 1) for i in range(4)])

    def across(v):
        return lax.ppermute(v, "latent", [(i, i ^ 2) for i in range(4)])

    def other_layer(v):
        return lax.ppermute(v, "layer", [(0, 1), (1, 0)])

    own = resid_in[0].T
    far = across(own)
    near = partner(own)
    parts = encode_first(own, near, clt_gain, enc_b, enc_w[0])
    far_near = partner(far)
    ahead = pick(dec_next.shape[1], 768)
    lat, head = encode_last(far, far_near, *parts, enc_w.shape[1], dec_next, ahead)

    def to_partner(snd, pairs):
        return lax.ppermute(snd, both, [(i, i ^ 1) for i in pairs])

    def to_chip(sent, pairs):
        return lax.ppermute(sent, both, [(i, i ^ 2) for i in pairs])

    same, frozen = dec_same[0], frozen_sum.T
    every = range(8)
    snd, oth, q_own, head = decode(lat, None, head, dec_next, lat, True, ((same, ahead),))
    q_got = to_partner(snd, every)
    done, head = decode_head(lat, head, same, snd, pick(same.shape[1] - ahead, 512))
    q_sent = next_send(oth, q_got)
    q_back = to_chip(q_sent, every)
    loads = ((frozen, frozen.shape[1]),)
    snd, oth, own, frozen, lat_out = decode(lat, done, head, same, snd, False, loads, True)
    got = to_partner(snd, every)
    sents = send_sum(oth, got)
    backs = [to_chip(sent, every) for sent in sents]
    normed = []
    for i, back in enumerate(backs):
        total, sent = layer_sum(i, own, got, back, q_own, q_got, q_back)
        normed.append(mix(i, total, other_layer(sent), frozen, mlp_gain))
    w_gate, w_up, w_down = resident(w_gate), resident(w_up), resident(w_down)
    n_near = [partner(v) for v in normed]
    n_far = [across(v) for v in normed]
    q_here = other_layer(next_sum(q_own, q_got, q_back))
    recon = recon_sum(own, got, q_here, backs)
    g, u, nsq = mlp_half(normed, n_near, w_gate, w_up, True, (), layers)
    n_far_near = [partner(v) for v in n_far]
    snd, keep = mlp_half(n_far, n_far_near, w_gate, w_up, False, (g, u, nsq, w_down), layers)
    got = partner(snd)
    kept, to_y, to_x, to_d = fold(keep, got)
    r_d = lax.ppermute(to_d, both, [(i, i ^ 6) for i in range(8)])
    r_x = other_layer(to_x)
    r_y = across(to_y)
    out = last_sum(kept, r_x, r_y, r_d)
    return (lat_out[None], recon.T[None], out.T)


def passed_along(block, axis, distance):
    devices = range(lax.axis_size(axis))
    route = [(i - distance, i) for i in devices if i - distance in devices]
    return lax.ppermute(block, axis, route)


def swapped_with(value, axis, stride):
    mask = 2**stride
    pairs = [(source, source ^ mask) for source in range(lax.axis_size(axis))]
    return lax.ppermute(value, axis, pairs)


def general(
    resid_in, clt_gain, enc_w, enc_b, dec_same, dec_next, frozen_sum, mlp_gain, w_gate, w_up, w_down
):
    own_rows = resid_in[0]
    feats = enc_w.shape[1]
    own_values = own_rows.astype(F32)
    squares = lax.psum(jnp.sum(own_values * own_values, axis=1, keepdims=True), "latent")
    gated = (lax.all_gather(own_rows, "latent", axis=1, tiled=True).astype(F32) * clt_gain[0]).astype(BF)
    projected = jnp.dot(gated, enc_w[0], preferred_element_type=F32)
    inv_scale = lax.rsqrt(squares / feats + 1e-06)
    lat_act = jnp.maximum(inv_scale * projected + enc_b[0], 0.0).astype(BF)
    is_first = lax.axis_index("layer") == 0
    own_term = jnp.dot(lat_act, dec_same[0], preferred_element_type=F32)
    arrived = passed_along(lat_act, "layer", 1)
    target_term = own_term + jnp.dot(arrived, dec_next, preferred_element_type=F32)
    own_sum = lax.psum_scatter(target_term, "latent", scatter_dimension=1, tiled=True)
    other_sum = swapped_with(own_sum, "layer", 0)
    recon_zero = jnp.where(is_first, own_sum, other_sum)
    recon_one = jnp.where(is_first, other_sum, own_sum)
    recon = own_sum.astype(BF)[None]
    mixed = frozen_sum.astype(F32) + recon_zero + recon_one
    normed = (mixed * mlp_gain).astype(BF)
    mixed_squares = lax.psum(jnp.sum(mixed * mixed, axis=1, keepdims=True), "latent")
    rows = lax.all_gather(normed, "latent", axis=1, tiled=True)
    gate_raw = jnp.dot(rows, w_gate, preferred_element_type=F32)
    up_raw = jnp.dot(rows, w_up, preferred_element_type=F32)
    row_scale = lax.rsqrt(mixed_squares / feats + 1e-06)
    hidden = (jax.nn.gelu(row_scale * gate_raw, approximate=True) * (row_scale * up_raw)).astype(BF)
    partials = jnp.dot(hidden, w_down, preferred_element_type=F32)
    mlp_out = lax.psum_scatter(
        partials, ("layer", "latent"), scatter_dimension=1, tiled=True
    ).astype(BF)
    return (lat_act[None], recon, mlp_out)


def solution(mesh):
    in_specs = (
        P("layer", "token", "latent"),
        P("layer", None),
        P("layer", None, "latent"),
        P("layer", "latent"),
        P("layer", "latent", None),
        P("latent", None),
        P("token", "latent"),
        P("latent"),
        P(None, ("layer", "latent")),
        P(None, ("layer", "latent")),
        P(("layer", "latent"), None),
    )
    out_specs = (
        P("layer", "token", "latent"),
        P("layer", "token", "latent"),
        P("token", ("layer", "latent")),
    )
    small = mesh.shape["layer"] == 2 and mesh.shape["latent"] == 4
    return jax.shard_map(
        blocked if small else general, mesh=mesh, in_specs=in_specs, out_specs=out_specs, check_vma=False
    )
```

```python
import functools

import jax
import jax.numpy as jnp
from jax import lax
from jax.experimental import pallas as pl
from jax.experimental.pallas import tpu as pltpu
from jax.sharding import PartitionSpec as P


BF = jnp.bfloat16
F32 = jnp.float32
VMEM = pl.BlockSpec(memory_space=pltpu.VMEM)
HBM = pl.BlockSpec(memory_space=pltpu.HBM)
ANY = pl.BlockSpec(memory_space=pl.ANY)
TAIL = 16
PARTS = 3
TRANSFER = 4 << 30


def dot_cols(x_km, w_kn):
    return lax.dot_general(x_km, w_kn, (((0,), (0,)), ((), ())), preferred_element_type=F32)


def whereabouts():
    place = lax.axis_index("latent")
    return place & 1, place >> 1, lax.axis_index("layer")


def in_block(work):
    pl.when(lax.axis_index("latent") >= 0)(work)


def column_of(row, width):
    n = row.shape[1]
    block = jnp.broadcast_to(row, (128, n)).T
    return jnp.concatenate([block] * (width // 128), axis=1)


def call(kernel, out_shapes, scratch, args, specs, flops, limit, out_specs=None):
    return pl.pallas_call(
        kernel,
        out_shape=out_shapes,
        in_specs=specs,
        out_specs=[VMEM] * len(out_shapes) if out_specs is None else out_specs,
        scratch_shapes=scratch,
        cost_estimate=pl.CostEstimate(flops=flops, transcendentals=0, bytes_accessed=0),
        compiler_params=pltpu.CompilerParams(vmem_limit_bytes=limit << 20),
    )(*args)


def in_hbm(array):
    return pltpu.with_memory_space_constraint(array, pltpu.HBM)


def resident(weights):
    return pltpu.with_memory_space_constraint(weights, pltpu.VMEM)


def pick(total, wanted):
    size = wanted - wanted % 128
    while size > 128 and total % size:
        size -= 128
    return size if total % size == 0 else total


def encode_first(own, other, gain, bias, enc):
    width, tokens = own.shape
    _, lats = enc.shape
    half = 2 * width
    tn = pick(lats, 1024)
    steps = lats // tn
    ahead = 3

    def kernel(
        own_ref, other_ref, gain_ref, bias_ref, enc_ref,
        acc_ref, sq_ref, gain_out, bias_out, rest_ref,
        xg, xown, gbuf, grest, wbuf, sems, small
    ):
        core, side, _ = whereabouts()
        mine = pl.multiple_of(side * half, half)
        others = pl.multiple_of((1 - side) * half, half)
        loads = [
            pltpu.make_async_copy(own_ref, xown, small.at[0]),
            pltpu.make_async_copy(gain_ref.at[:, pl.ds(mine, half)], gbuf, small.at[1]),
        ]
        later = [
            pltpu.make_async_copy(gain_ref.at[:, pl.ds(others, half)], grest, small.at[2]),
            pltpu.make_async_copy(bias_ref, bias_out, small.at[3]),
        ]

        def weights(j):
            cols = pl.ds(j % steps * tn, tn)
            if j < steps:
                return pltpu.make_async_copy(enc_ref.at[pl.ds(mine, half), cols], wbuf.at[:, cols], sems.at[j])
            return pltpu.make_async_copy(enc_ref.at[pl.ds(others, half), cols], rest_ref.at[:, cols], sems.at[j])

        for c in loads:
            c.start()
        for j in range(ahead):
            weights(j).start()
        for c in later:
            c.start()
        for c in loads:
            c.wait()

        def gather():
            xg[pl.ds(pl.multiple_of(core * width, width), width), :] = xown[...]
            xg[pl.ds(pl.multiple_of((1 - core) * width, width), width), :] = other_ref[...]
            values = xg[...].astype(F32)
            squares = jnp.sum(values * values, axis=0, keepdims=True)
            xg[...] = (values * column_of(gbuf[...], tokens)).astype(BF)
            sq_ref[...] = jnp.broadcast_to(squares, sq_ref.shape)

        def apply(j):
            cols = pl.ds(j * tn, tn)
            acc_ref[:, cols] = dot_cols(xg[...], wbuf[:, cols])

        in_block(gather)
        for j in range(2 * steps):
            weights(j).wait()
            if j + ahead < 2 * steps:
                weights(j + ahead).start()
            if j < steps:
                in_block(functools.partial(apply, j))
        for c in later:
            c.wait()
        gain_out[...] = column_of(grest[...], tokens)

    shape = jax.ShapeDtypeStruct
    outs = [
        shape((tokens, lats), F32),
        shape((8, tokens), F32),
        shape((half, tokens), F32),
        shape((1, lats), F32),
        shape((half, lats), BF),
    ]
    scratch = [
        pltpu.VMEM((half, tokens), BF),
        pltpu.VMEM((width, tokens), BF),
        pltpu.VMEM((1, half), F32),
        pltpu.VMEM((1, half), F32),
        pltpu.VMEM((half, lats), BF),
        pltpu.SemaphoreType.DMA((2 * steps,)),
        pltpu.SemaphoreType.DMA((4,)),
    ]
    specs = [HBM, VMEM, HBM, HBM, HBM]
    return call(
        kernel,
        outs,
        scratch,
        (in_hbm(own), other, in_hbm(gain), in_hbm(bias), in_hbm(enc)),
        specs,
        8 * tokens * half * lats,
        16,
    )


def encode_more(block, acc, sq, gain, rest, near, load, bias=None, feats=0):
    width, tokens = block.shape
    lats = rest.shape[1]
    tn = pick(lats, 1024)
    dec, load_at, load_cols = load
    last = bias is not None

    def kernel(block_ref, acc_ref, sq_ref, gain_ref, rest_ref, dec_ref, *refs):
        if last:
            bias_ref, out_ref, head_ref, xg, sems, scale = refs
        else:
            out_ref, sq_out, head_ref, xg, sems = refs
        load = pltpu.make_async_copy(dec_ref.at[:, pl.ds(load_at, load_cols)], head_ref, sems.at[0])
        load.start()
        core = whereabouts()[0]
        row = pl.multiple_of((1 - core if near else core) * width, width)

        def work():
            values = block_ref[...].astype(F32)
            squares = jnp.sum(values * values, axis=0, keepdims=True) + sq_ref[0:1, :]
            xg[...] = (values * gain_ref[pl.ds(row, width), :]).astype(BF)
            if last:
                scale[...] = jnp.broadcast_to(lax.rsqrt(squares / feats + 1e-06), (128, tokens)).T
            else:
                sq_out[...] = jnp.broadcast_to(squares, sq_out.shape)
            for j in range(lats // tn):
                cols = pl.ds(j * tn, tn)
                total = dot_cols(xg[...], rest_ref[pl.ds(row, width), cols]) + acc_ref[:, cols]
                if last:
                    out_ref[:, cols] = jnp.maximum(scale[:, 0:1] * total + bias_ref[:, cols], 0.0).astype(BF)
                else:
                    out_ref[:, cols] = total

        in_block(work)
        load.wait()

    shape = jax.ShapeDtypeStruct
    head = shape((dec.shape[0], load_cols), BF)
    scratch = [pltpu.VMEM((width, tokens), BF), pltpu.SemaphoreType.DMA((1,))]
    args = (block, acc, sq, gain, rest, in_hbm(dec))
    specs = [VMEM] * 5 + [HBM]
    if last:
        args, specs = args + (bias,), specs + [VMEM]
        outs = [shape((tokens, lats), BF), head]
        scratch += [pltpu.VMEM((tokens, 128), F32)]
    else:
        outs = [shape((tokens, lats), F32), shape((8, tokens), F32), head]
    return call(kernel, outs, scratch, args, specs, 2 * tokens * width * lats, 8)


def decode_head(lat, head, dec, after, more):
    tokens, lats = lat.shape
    cols = head.shape[1]

    def kernel(lat_ref, after_ref, head_ref, dec_ref, yt_ref, more_ref, sems):
        load = pltpu.make_async_copy(dec_ref.at[:, pl.ds(cols, more)], more_ref, sems.at[0])
        load.start()

        def work():
            yt_ref[...] = jnp.dot(lat_ref[...], head_ref[...], preferred_element_type=F32).T

        in_block(work)
        load.wait()

    outs = [jax.ShapeDtypeStruct((cols, tokens), F32), jax.ShapeDtypeStruct((lats, more), BF)]
    args = (lat, after, head, in_hbm(dec))
    return call(
        kernel, outs, [pltpu.SemaphoreType.DMA((1,))], args, [VMEM, ANY, VMEM, HBM],
        2 * tokens * lats * cols, 5,
    )


def decode(lat, done, heads, dec, after, only_first, loads=()):
    tokens, lats = lat.shape
    feats = dec.shape[1]
    ready = 0 if done is None else done.shape[0]
    widths = [h.shape[1] for h in heads]
    loaded = ready + sum(widths)
    block = feats // 4
    size = pick(feats - loaded, 512)
    tails = [(at, size) for at in range(loaded, feats, size)]
    pieces = [(i, at, pick(w, 256)) for i, w in enumerate(widths) for at in range(0, w, pick(w, 256))]
    rows_of = lats // 2

    def kernel(lat_ref, after_ref, dec_ref, *rest):
        head_refs, rest = rest[: len(heads)], rest[len(heads) :]
        if ready:
            done_ref, *rest = rest
        load_refs, rest = rest[: len(loads)], rest[len(loads) :]
        far_ref, near_ref, oth_ref, own_ref, *rest = rest
        loaded_refs, rest = rest[: len(loads)], rest[len(loads) :]
        wbuf, yt, wsems, sems = rest
        copies = [
            pltpu.make_async_copy(source.at[:, pl.ds(0, cols)], target, sems.at[i])
            for i, (source, target, (_, cols)) in enumerate(zip(load_refs, loaded_refs, loads))
        ]
        core, side, layer = whereabouts()

        def weights(i):
            at, size = tails[i]
            return [
                pltpu.make_async_copy(
                    dec_ref.at[pl.ds(k * rows_of, rows_of), pl.ds(at, size)],
                    wbuf.at[pl.ds(k * rows_of, rows_of), pl.ds(at - loaded, size)],
                    wsems.at[i, k],
                )
                for k in range(2)
            ]

        def rows(h, c):
            return pl.ds(pl.multiple_of((2 * h + c) * block, block), block)

        def apply(target, weights_of):
            yt[target, :] = jnp.dot(lat_ref[...], weights_of(), preferred_element_type=F32).T

        def share():
            far_ref[...] = yt[rows(1 - side, 1 - core), :].astype(BF)
            near_ref[...] = yt[rows(side, 1 - core), :].astype(BF)
            oth_ref[...] = yt[rows(1 - side, core), :]
            own_ref[...] = yt[rows(side, core), :]

        def bring():
            yt[pl.ds(0, ready), :] = done_ref[...]

        def work():
            pending = [c for i in range(len(tails)) for c in weights(i)]

            def start(count):
                for _ in range(min(count, len(pending))):
                    pending.pop(0).start()

            start(2)
            if ready:
                in_block(bring)
            target = ready
            for i, at, size in pieces:
                cols = pl.ds(at, size)
                in_block(
                    functools.partial(apply, pl.ds(target, size), lambda i=i, cols=cols: head_refs[i][:, cols])
                )
                target += size
                start(1)
            for i, (at, size) in enumerate(tails):
                for c in weights(i):
                    c.wait()
                start(2)
                if i == max(0, len(tails) - 2):
                    start(len(pending))
                    for c in copies:
                        c.start()
                cols = pl.ds(at - loaded, size)
                in_block(
                    functools.partial(apply, pl.ds(at, size), lambda cols=cols: wbuf[:, cols])
                )
            in_block(share)

        if only_first:
            pl.when(layer == 0)(work)

            @pl.when(layer != 0)
            def _():
                for c in copies:
                    c.start()
        else:
            work()
        for c in copies:
            c.wait()

    shape = jax.ShapeDtypeStruct
    outs = [shape((block, tokens), BF)] * 2 + [shape((block, tokens), F32)] * 2
    outs += [shape((v.shape[0], cols), v.dtype) for v, cols in loads]
    scratch = [
        pltpu.VMEM((lats, feats - loaded), BF),
        pltpu.VMEM((feats, tokens), F32),
        pltpu.SemaphoreType.DMA((len(tails), 2)),
        pltpu.SemaphoreType.DMA((max(1, len(loads)),)),
    ]
    args = (lat, after, in_hbm(dec), *heads) + ((done,) if ready else ()) + tuple(in_hbm(v) for v, _ in loads)
    specs = [VMEM, ANY, HBM] + [VMEM] * (len(heads) + (ready > 0)) + [HBM] * len(loads)
    limit = 8 + lats * (feats - loaded) * 2 // (1 << 20)
    return call(kernel, outs, scratch, args, specs, 2 * tokens * lats * (feats - ready), limit)


def part_of(rows, i):
    return pl.ds(i * (rows // PARTS), rows // PARTS)


def send_sum(oth, got):
    rows, tokens = oth.shape

    def kernel(oth_ref, got_ref, *out_refs):
        for i, out_ref in enumerate(out_refs):
            at = part_of(rows, i)
            out_ref[...] = (oth_ref[at, :] + got_ref[at, :].astype(F32)).astype(BF)

    outs = [jax.ShapeDtypeStruct((rows // PARTS, tokens), BF)] * PARTS
    return call(kernel, outs, [], (oth, got), [VMEM] * 2, TRANSFER, 4)


def next_send(oth, got):
    def kernel(oth_ref, got_ref, out_ref):
        out_ref[...] = (oth_ref[...] + got_ref[...].astype(F32)).astype(BF)

    return call(kernel, [jax.ShapeDtypeStruct(oth.shape, BF)], [], (oth, got), [VMEM] * 2, oth.size, 4)[0]


def layer_sum(i, own, got, back, q_own, q_got, q_back):
    rows, tokens = own.shape
    at = part_of(rows, i)

    def kernel(own_ref, got_ref, back_ref, qo_ref, qg_ref, qb_ref, sum_ref, out_ref):
        total = own_ref[at, :] + got_ref[at, :].astype(F32) + back_ref[...].astype(F32)
        sum_ref[...] = total

        @pl.when(whereabouts()[2] == 0)
        def _():
            extra = qo_ref[at, :] + qg_ref[at, :].astype(F32) + qb_ref[at, :].astype(F32)
            sum_ref[...] = sum_ref[...] + extra

        out_ref[...] = sum_ref[...].astype(BF)

    shape = jax.ShapeDtypeStruct
    outs = [shape((rows // PARTS, tokens), F32), shape((rows // PARTS, tokens), BF)]
    args = (own, got, back, q_own, q_got, q_back)
    return call(kernel, outs, [], args, [VMEM] * 6, TRANSFER, 5)


def next_sum(own, got, back):
    def kernel(own_ref, got_ref, back_ref, out_ref):
        out_ref[...] = (own_ref[...] + got_ref[...].astype(F32) + back_ref[...].astype(F32)).astype(BF)

    outs = [jax.ShapeDtypeStruct(own.shape, BF)]
    return call(kernel, outs, [], (own, got, back), [VMEM] * 3, own.size, 4)[0]


def recon_sum(own, got, extra, backs):
    rows, _ = own.shape

    def kernel(own_ref, got_ref, extra_ref, *refs):
        *back_refs, out_ref = refs
        from_first = whereabouts()[2] == 1
        for i, back_ref in enumerate(back_refs):
            at = part_of(rows, i)
            total = own_ref[at, :] + got_ref[at, :].astype(F32) + back_ref[...].astype(F32)
            extra = jnp.where(from_first, extra_ref[at, :].astype(F32), 0.0)
            out_ref[at, :] = (total + extra).astype(BF)

    outs = [jax.ShapeDtypeStruct(own.shape, BF)]
    args = (own, got, extra) + tuple(backs)
    return call(kernel, outs, [], args, [VMEM] * (3 + len(backs)), own.size, 5)[0]


def mix(i, target, other, frozen, gain):
    part, tokens = target.shape
    at = pl.ds(i * part, part)

    def kernel(t_ref, o_ref, f_ref, g_ref, out_ref):
        mixed = f_ref[at, :].astype(F32) + t_ref[...] + o_ref[...].astype(F32)
        gains = column_of(g_ref[...][None, :], tokens)
        out_ref[pl.ds(0, part), :] = (mixed * gains[i * part : (i + 1) * part, :]).astype(BF)
        squares = jnp.sum(mixed * mixed, axis=0, keepdims=True)
        high = squares.astype(BF).astype(F32)
        rest = squares - high
        mid = rest.astype(BF).astype(F32)
        low = rest - mid
        row = lax.broadcasted_iota(jnp.int32, (TAIL, tokens), 0)
        tail = jnp.where(row == 0, high, jnp.where(row == 1, mid, jnp.where(row == 2, low, 0.0)))
        out_ref[pl.ds(part, TAIL), :] = tail.astype(BF)

    outs = [jax.ShapeDtypeStruct((part + TAIL, tokens), BF)]
    return call(kernel, outs, [], (target, other, frozen, gain), [VMEM] * 4, TRANSFER, 5)[0]


def fold(keep, got, stays):
    count, piece, tokens = keep.shape

    def kernel(keep_ref, got_ref, *out_refs):
        for i, out_ref in enumerate(out_refs):
            out_ref[...] = (keep_ref[i] + got_ref[i].astype(F32)).astype(out_ref.dtype)

    outs = [jax.ShapeDtypeStruct((piece, tokens), F32 if stays and i == 0 else BF) for i in range(count)]
    return call(kernel, outs, [], (keep, got), [VMEM] * 2, count * piece * tokens, 6)


def last_sum(own, *others):
    def kernel(own_ref, *refs):
        *other_refs, out_ref = refs
        total = own_ref[...]
        for r in other_refs:
            total = total + r[...].astype(F32)
        out_ref[...] = total.astype(BF)

    outs = [jax.ShapeDtypeStruct(own.shape, BF)]
    return call(kernel, outs, [], (own,) + others, [VMEM] * (1 + len(others)), own.size, 4)[0]


def down_half(hidden_ref, wd_ref, snd_ref, keep_ref, yt, far):
    count, piece, _ = keep_ref.shape
    half = 2 * count * piece
    core, side, layer = whereabouts()
    col = pl.multiple_of((1 - layer if far else layer) * half, half)
    yt[...] = jnp.dot(hidden_ref[...], wd_ref[:, pl.ds(col, half)], preferred_element_type=F32).T
    for i in range(count):
        at = (side ^ i) * 2
        snd_ref[i] = yt[pl.ds(pl.multiple_of((at + 1 - core) * piece, piece), piece), :].astype(BF)
        keep_ref[i] = yt[pl.ds(pl.multiple_of((at + core) * piece, piece), piece), :]


def mlp_down(hidden, w_down, after, layers):
    tokens, units = hidden.shape
    feats = w_down.shape[1]
    piece = feats // (4 * layers)

    def kernel(hidden_ref, wd_ref, after_ref, snd_ref, keep_ref, yt):
        down_half(hidden_ref, wd_ref, snd_ref, keep_ref, yt, False)

    shape = jax.ShapeDtypeStruct
    outs = [shape((2, piece, tokens), BF), shape((2, piece, tokens), F32)]
    scratch = [pltpu.VMEM((feats // layers, tokens), F32)]
    args = (hidden, w_down, after)
    return call(kernel, outs, scratch, args, [VMEM, VMEM, ANY], tokens * units * feats, 6)


def mlp_half(owns, others, w_gate, w_up, first, extra, layers):
    part, tokens = owns[0].shape[0] - TAIL, owns[0].shape[1]
    width = part * PARTS
    half = 2 * width
    feats, units = w_gate.shape
    piece = feats // (4 * layers)

    def kernel(*rest):
        own_refs, other_refs, (wg_ref, wu_ref, *rest) = rest[:PARTS], rest[PARTS : 2 * PARTS], rest[2 * PARTS :]
        if first:
            lat_ref, g_ref, u_ref, sq_ref, lat_out, xg, sems = rest
            write = pltpu.make_async_copy(lat_ref, lat_out, sems.at[0])
            write.start()
        else:
            g_in, u_in, sq_in, wd_ref, hidden_ref, snd_ref, keep_ref, xg, yt = rest
        core, side, _ = whereabouts()
        row = side if first else 1 - side
        row = pl.multiple_of(row * half, half)

        def gather():
            squares = jnp.zeros((1, tokens), F32)
            for refs, c in ((own_refs, core), (other_refs, 1 - core)):
                for i, ref in enumerate(refs):
                    xg[pl.ds(pl.multiple_of(c * width + i * part, part), part), :] = ref[pl.ds(0, part), :]
                    squares += jnp.sum(ref[pl.ds(part, TAIL), :].astype(F32), axis=0, keepdims=True)
            gate = dot_cols(xg[...], wg_ref[pl.ds(row, half), :])
            up = dot_cols(xg[...], wu_ref[pl.ds(row, half), :])
            return squares, gate, up

        def work():
            squares, gate, up = gather()
            g_ref[...] = gate
            u_ref[...] = up
            sq_ref[...] = jnp.broadcast_to(squares, sq_ref.shape)

        if first:
            in_block(work)
            write.wait()
            return
        squares, gate, up = gather()
        total = squares + sq_in[0:1, :]
        scale = jnp.broadcast_to(lax.rsqrt(total / feats + 1e-06), (128, tokens)).T[:, 0:1]
        gate = scale * (gate + g_in[...])
        up = scale * (up + u_in[...])
        hidden_ref[...] = (jax.nn.gelu(gate, approximate=True) * up).astype(BF)
        down_half(hidden_ref, wd_ref, snd_ref, keep_ref, yt, True)

    shape = jax.ShapeDtypeStruct
    scratch = [pltpu.VMEM((half, tokens), BF)]
    out_specs = None
    if first:
        lat = extra[0]
        outs = [shape((tokens, units), F32), shape((tokens, units), F32), shape((8, tokens), F32)]
        outs += [shape(lat.shape, lat.dtype)]
        out_specs = [VMEM] * 3 + [HBM]
        scratch += [pltpu.SemaphoreType.DMA((1,))]
    else:
        outs = [shape((tokens, units), BF), shape((2, piece, tokens), BF), shape((2, piece, tokens), F32)]
        scratch += [pltpu.VMEM((feats // layers, tokens), F32)]
    args = (*owns, *others, w_gate, w_up) + extra
    flops = 4 * tokens * half * units + (0 if first else tokens * units * feats)
    return call(kernel, outs, scratch, args, [VMEM] * len(args), flops, 6 if first else 12, out_specs)


def blocked(
    resid_in, clt_gain, enc_w, enc_b, dec_same, dec_next, frozen_sum, mlp_gain, w_gate, w_up, w_down
):
    return blocked_steps(
        resid_in, clt_gain, enc_w, enc_b, dec_same, dec_next, frozen_sum, mlp_gain, w_gate, w_up, w_down
    )


def blocked_steps(
    resid_in, clt_gain, enc_w, enc_b, dec_same, dec_next, frozen_sum, mlp_gain, w_gate, w_up, w_down
):
    layers = lax.axis_size("layer")
    both = ("layer", "latent")

    def partner(v):
        return lax.ppermute(v, "latent", [(i, i ^ 1) for i in range(4)])

    def across(v):
        return lax.ppermute(v, "latent", [(i, i ^ 2) for i in range(4)])

    def other_layer(v):
        return lax.ppermute(v, "layer", [(0, 1), (1, 0)])

    own = resid_in[0].T
    far = across(own)
    near = partner(own)
    parts = encode_first(own, near, clt_gain, enc_b, enc_w[0])
    far_near = partner(far)
    acc, sq, gains, bias, rest = parts
    ahead = pick(dec_next.shape[1], 768)
    more = pick(dec_next.shape[1] - ahead, 512)
    acc, sq, head = encode_more(far, acc, sq, gains, rest, False, (dec_next, 0, more))
    lat, head_2 = encode_more(
        far_near, acc, sq, gains, rest, True, (dec_next, more, ahead), bias, enc_w.shape[1]
    )

    def to_partner(snd, pairs):
        return lax.ppermute(snd, both, [(i, i ^ 1) for i in pairs])

    def to_chip(sent, pairs):
        return lax.ppermute(sent, both, [(i, i ^ 2) for i in pairs])

    same, frozen = dec_same[0], frozen_sum.T
    every = range(8)
    snd, snd_near, oth, q_own, head = decode(lat, None, [head, head_2], dec_next, lat, True, ((same, ahead),))
    got = to_partner(snd, every)
    done, head = decode_head(lat, head, same, snd, pick(same.shape[1] - ahead, 512))
    q_back = to_chip(next_send(oth, got), every)
    q_got = to_partner(snd_near, every)
    loads = ((frozen, frozen.shape[1]),)
    snd, snd_near, oth, own, frozen = decode(lat, done, [head], same, snd, False, loads)
    got = to_partner(snd, every)
    sents = send_sum(oth, got)
    backs = [to_chip(sent, every) for sent in sents]
    got = to_partner(snd_near, every)
    normed = []
    for i, back in enumerate(backs):
        total, sent = layer_sum(i, own, got, back, q_own, q_got, q_back)
        normed.append(mix(i, total, other_layer(sent), frozen, mlp_gain))
    w_gate, w_up, w_down = resident(w_gate), resident(w_up), resident(w_down)
    n_near = [partner(v) for v in normed]
    n_far = [across(v) for v in normed]
    q_here = other_layer(next_sum(q_own, q_got, q_back))
    recon = recon_sum(own, got, q_here, backs)
    g, u, nsq, lat_out = mlp_half(normed, n_near, w_gate, w_up, True, (lat,), layers)
    n_far_near = [partner(v) for v in n_far]
    hidden, snd, keep = mlp_half(n_far, n_far_near, w_gate, w_up, False, (g, u, nsq, w_down), layers)
    got = partner(snd)
    snd, near_keep = mlp_down(hidden, w_down, snd, layers)
    near_got = partner(snd)
    to_x, to_d = fold(keep, got, False)
    r_d = lax.ppermute(to_d, both, [(i, i ^ 6) for i in range(8)])
    r_x = other_layer(to_x)
    kept, to_y = fold(near_keep, near_got, True)
    r_y = across(to_y)
    out = last_sum(kept, r_x, r_y, r_d)
    return (lat_out[None], recon.T[None], out.T)


def passed_along(block, axis, distance):
    devices = range(lax.axis_size(axis))
    route = [(i - distance, i) for i in devices if i - distance in devices]
    return lax.ppermute(block, axis, route)


def swapped_with(value, axis, stride):
    mask = 2**stride
    pairs = [(source, source ^ mask) for source in range(lax.axis_size(axis))]
    return lax.ppermute(value, axis, pairs)


def general(
    resid_in, clt_gain, enc_w, enc_b, dec_same, dec_next, frozen_sum, mlp_gain, w_gate, w_up, w_down
):
    own_rows = resid_in[0]
    feats = enc_w.shape[1]
    own_values = own_rows.astype(F32)
    squares = lax.psum(jnp.sum(own_values * own_values, axis=1, keepdims=True), "latent")
    gated = (lax.all_gather(own_rows, "latent", axis=1, tiled=True).astype(F32) * clt_gain[0]).astype(BF)
    projected = jnp.dot(gated, enc_w[0], preferred_element_type=F32)
    inv_scale = lax.rsqrt(squares / feats + 1e-06)
    lat_act = jnp.maximum(inv_scale * projected + enc_b[0], 0.0).astype(BF)
    is_first = lax.axis_index("layer") == 0
    own_term = jnp.dot(lat_act, dec_same[0], preferred_element_type=F32)
    arrived = passed_along(lat_act, "layer", 1)
    target_term = own_term + jnp.dot(arrived, dec_next, preferred_element_type=F32)
    own_sum = lax.psum_scatter(target_term, "latent", scatter_dimension=1, tiled=True)
    other_sum = swapped_with(own_sum, "layer", 0)
    recon_zero = jnp.where(is_first, own_sum, other_sum)
    recon_one = jnp.where(is_first, other_sum, own_sum)
    recon = own_sum.astype(BF)[None]
    mixed = frozen_sum.astype(F32) + recon_zero + recon_one
    normed = (mixed * mlp_gain).astype(BF)
    mixed_squares = lax.psum(jnp.sum(mixed * mixed, axis=1, keepdims=True), "latent")
    rows = lax.all_gather(normed, "latent", axis=1, tiled=True)
    gate_raw = jnp.dot(rows, w_gate, preferred_element_type=F32)
    up_raw = jnp.dot(rows, w_up, preferred_element_type=F32)
    row_scale = lax.rsqrt(mixed_squares / feats + 1e-06)
    hidden = (jax.nn.gelu(row_scale * gate_raw, approximate=True) * (row_scale * up_raw)).astype(BF)
    partials = jnp.dot(hidden, w_down, preferred_element_type=F32)
    mlp_out = lax.psum_scatter(
        partials, ("layer", "latent"), scatter_dimension=1, tiled=True
    ).astype(BF)
    return (lat_act[None], recon, mlp_out)


def solution(mesh):
    in_specs = (
        P("layer", "token", "latent"),
        P("layer", None),
        P("layer", None, "latent"),
        P("layer", "latent"),
        P("layer", "latent", None),
        P("latent", None),
        P("token", "latent"),
        P("latent"),
        P(None, ("layer", "latent")),
        P(None, ("layer", "latent")),
        P(("layer", "latent"), None),
    )
    out_specs = (
        P("layer", "token", "latent"),
        P("layer", "token", "latent"),
        P("token", ("layer", "latent")),
    )
    small = mesh.shape["layer"] == 2 and mesh.shape["latent"] == 4
    return jax.shard_map(
        blocked if small else general, mesh=mesh, in_specs=in_specs, out_specs=out_specs, check_vma=False
    )
```

```python
import functools

import jax
import jax.numpy as jnp
from jax import lax
from jax.experimental import pallas as pl
from jax.experimental.pallas import tpu as pltpu
from jax.sharding import PartitionSpec as P


BF = jnp.bfloat16
F32 = jnp.float32
VMEM = pl.BlockSpec(memory_space=pltpu.VMEM)
HBM = pl.BlockSpec(memory_space=pltpu.HBM)
ANY = pl.BlockSpec(memory_space=pl.ANY)
TAIL = 16
PARTS = 3
TRANSFER = 3 << 30


def dot_cols(x_km, w_kn):
    return lax.dot_general(x_km, w_kn, (((0,), (0,)), ((), ())), preferred_element_type=F32)


def whereabouts():
    place = lax.axis_index("latent")
    return place & 1, place >> 1, lax.axis_index("layer")


def in_block(work):
    pl.when(lax.axis_index("latent") >= 0)(work)


def column_of(row, width):
    n = row.shape[1]
    block = jnp.broadcast_to(row, (128, n)).T
    return jnp.concatenate([block] * (width // 128), axis=1)


def call(kernel, out_shapes, scratch, args, specs, flops, limit, out_specs=None):
    return pl.pallas_call(
        kernel,
        out_shape=out_shapes,
        in_specs=specs,
        out_specs=[VMEM] * len(out_shapes) if out_specs is None else out_specs,
        scratch_shapes=scratch,
        cost_estimate=pl.CostEstimate(flops=flops, transcendentals=0, bytes_accessed=0),
        compiler_params=pltpu.CompilerParams(vmem_limit_bytes=limit << 20),
    )(*args)


def in_hbm(array):
    return pltpu.with_memory_space_constraint(array, pltpu.HBM)


def resident(weights):
    return pltpu.with_memory_space_constraint(weights, pltpu.VMEM)


def pick(total, wanted):
    size = wanted - wanted % 128
    while size > 128 and total % size:
        size -= 128
    return size if total % size == 0 else total


def encode_first(own, other, gain, bias, enc):
    width, tokens = own.shape
    _, lats = enc.shape
    half = 2 * width
    tn = pick(lats, 1024)
    steps = lats // tn
    ahead = 3

    def kernel(
        own_ref, other_ref, gain_ref, bias_ref, enc_ref,
        acc_ref, sq_ref, gain_out, bias_out, rest_ref,
        xg, xown, gbuf, grest, wbuf, sems, small
    ):
        core, side, _ = whereabouts()
        mine = pl.multiple_of(side * half, half)
        others = pl.multiple_of((1 - side) * half, half)
        loads = [
            pltpu.make_async_copy(own_ref, xown, small.at[0]),
            pltpu.make_async_copy(gain_ref.at[:, pl.ds(mine, half)], gbuf, small.at[1]),
        ]
        later = [
            pltpu.make_async_copy(gain_ref.at[:, pl.ds(others, half)], grest, small.at[2]),
            pltpu.make_async_copy(bias_ref, bias_out, small.at[3]),
        ]

        def weights(j):
            cols = pl.ds(j % steps * tn, tn)
            if j < steps:
                return pltpu.make_async_copy(enc_ref.at[pl.ds(mine, half), cols], wbuf.at[:, cols], sems.at[j])
            return pltpu.make_async_copy(enc_ref.at[pl.ds(others, half), cols], rest_ref.at[:, cols], sems.at[j])

        for c in loads:
            c.start()
        for j in range(ahead):
            weights(j).start()
        for c in later:
            c.start()
        for c in loads:
            c.wait()

        def gather():
            xg[pl.ds(pl.multiple_of(core * width, width), width), :] = xown[...]
            xg[pl.ds(pl.multiple_of((1 - core) * width, width), width), :] = other_ref[...]
            values = xg[...].astype(F32)
            squares = jnp.sum(values * values, axis=0, keepdims=True)
            xg[...] = (values * column_of(gbuf[...], tokens)).astype(BF)
            sq_ref[...] = jnp.broadcast_to(squares, sq_ref.shape)

        def apply(j):
            cols = pl.ds(j * tn, tn)
            acc_ref[:, cols] = dot_cols(xg[...], wbuf[:, cols])

        in_block(gather)
        for j in range(2 * steps):
            weights(j).wait()
            if j + ahead < 2 * steps:
                weights(j + ahead).start()
            if j < steps:
                in_block(functools.partial(apply, j))
        for c in later:
            c.wait()
        gain_out[...] = column_of(grest[...], tokens)

    shape = jax.ShapeDtypeStruct
    outs = [
        shape((tokens, lats), F32),
        shape((8, tokens), F32),
        shape((half, tokens), F32),
        shape((1, lats), F32),
        shape((half, lats), BF),
    ]
    scratch = [
        pltpu.VMEM((half, tokens), BF),
        pltpu.VMEM((width, tokens), BF),
        pltpu.VMEM((1, half), F32),
        pltpu.VMEM((1, half), F32),
        pltpu.VMEM((half, lats), BF),
        pltpu.SemaphoreType.DMA((2 * steps,)),
        pltpu.SemaphoreType.DMA((4,)),
    ]
    specs = [HBM, VMEM, HBM, HBM, HBM]
    return call(
        kernel,
        outs,
        scratch,
        (in_hbm(own), other, in_hbm(gain), in_hbm(bias), in_hbm(enc)),
        specs,
        8 * tokens * half * lats,
        16,
    )


def encode_more(block, acc, sq, gain, rest, near, loads, bias=None, feats=0):
    width, tokens = block.shape
    lats = rest.shape[1]
    tn = pick(lats, 1024)
    count = len(loads)
    last = bias is not None

    def kernel(block_ref, acc_ref, sq_ref, gain_ref, rest_ref, *refs):
        load_refs, refs = refs[:count], refs[count:]
        if last:
            bias_ref, out_ref, *refs = refs
        else:
            out_ref, sq_out, *refs = refs
        loaded_refs, (xg, sems, *scale_refs) = refs[:count], refs[count:]
        copies = [
            pltpu.make_async_copy(columns(source, load), target, sems.at[i])
            for i, (source, target, load) in enumerate(zip(load_refs, loaded_refs, loads))
        ]
        for c in copies:
            c.start()
        core = whereabouts()[0]
        row = pl.multiple_of((1 - core if near else core) * width, width)

        def work():
            values = block_ref[...].astype(F32)
            squares = jnp.sum(values * values, axis=0, keepdims=True) + sq_ref[0:1, :]
            xg[...] = (values * gain_ref[pl.ds(row, width), :]).astype(BF)
            if last:
                scale_refs[0][...] = jnp.broadcast_to(lax.rsqrt(squares / feats + 1e-06), (128, tokens)).T
            else:
                sq_out[...] = jnp.broadcast_to(squares, sq_out.shape)
            for j in range(lats // tn):
                cols = pl.ds(j * tn, tn)
                total = dot_cols(xg[...], rest_ref[pl.ds(row, width), cols]) + acc_ref[:, cols]
                if last:
                    out_ref[:, cols] = jnp.maximum(scale_refs[0][:, 0:1] * total + bias_ref[:, cols], 0.0).astype(BF)
                else:
                    out_ref[:, cols] = total

        in_block(work)
        for c in copies:
            c.wait()

    shape = jax.ShapeDtypeStruct
    heads = [shape((v.shape[0], cols), v.dtype) for v, _, _, cols in loads]
    scratch = [pltpu.VMEM((width, tokens), BF), pltpu.SemaphoreType.DMA((count,))]
    args = (block, acc, sq, gain, rest) + tuple(in_hbm(v) for v, *_ in loads)
    specs = [VMEM] * 5 + [HBM] * count
    if last:
        args, specs = args + (bias,), specs + [VMEM]
        outs = [shape((tokens, lats), BF)] + heads
        scratch += [pltpu.VMEM((tokens, 128), F32)]
    else:
        outs = [shape((tokens, lats), F32), shape((8, tokens), F32)] + heads
    return call(kernel, outs, scratch, args, specs, 2 * tokens * width * lats, 8)


def columns(ref, load):
    _, far, at, count = load
    if far is None:
        return ref
    side = whereabouts()[1]
    base = (1 - side if far else side) * (ref.shape[1] // 2) + at
    return ref.at[:, pl.ds(pl.multiple_of(base, 128), count)]


def decode(lat, done, heads, dec, after, far, only_first, stop, loads):
    tokens, lats = lat.shape
    half = dec.shape[1] // 2
    block = half // 2
    whole = stop == half
    ready = 0 if done is None else done.shape[0]
    widths = [h.shape[1] for h in heads]
    loaded = ready + sum(widths)
    left = stop - loaded
    rows_of = lats // 2

    def kernel(lat_ref, after_ref, dec_ref, *rest):
        head_refs, rest = rest[: len(heads)], rest[len(heads) :]
        if ready:
            done_ref, *rest = rest
        load_refs, rest = rest[: len(loads)], rest[len(loads) :]
        if whole:
            snd_ref, keep_ref, *rest = rest
        else:
            sums_ref, *rest = rest
        loaded_refs, rest = rest[: len(loads)], rest[len(loads) :]
        wbuf, wsems, sems, *rest = rest
        yt = rest[0] if whole else sums_ref
        copies = [
            pltpu.make_async_copy(columns(source, load), target, sems.at[i])
            for i, (source, target, load) in enumerate(zip(load_refs, loaded_refs, loads))
        ]
        core, _, layer = whereabouts()
        weights = columns(dec_ref, (None, far, loaded, left)) if left else None

        def fetch(k):
            rows = pl.ds(k * rows_of, rows_of)
            return pltpu.make_async_copy(weights.at[rows, :], wbuf.at[rows, :], wsems.at[k])

        def apply(at, size, weights_of):
            yt[pl.ds(at, size), :] = jnp.dot(lat_ref[...], weights_of[...], preferred_element_type=F32).T

        def bring():
            yt[pl.ds(0, ready), :] = done_ref[...]

        def share():
            snd_ref[...] = yt[pl.ds(pl.multiple_of((1 - core) * block, block), block), :].astype(BF)
            keep_ref[...] = yt[pl.ds(pl.multiple_of(core * block, block), block), :]

        def work():
            if left:
                for k in range(2):
                    fetch(k).start()
            for c in copies:
                c.start()
            if ready:
                in_block(bring)
            at = ready
            for i, width in enumerate(widths):
                in_block(functools.partial(apply, at, width, head_refs[i]))
                at += width
            if left:
                for k in range(2):
                    fetch(k).wait()
                in_block(functools.partial(apply, at, left, wbuf))
            if whole:
                in_block(share)

        if only_first:
            pl.when(layer == 0)(work)

            @pl.when(layer != 0)
            def _():
                for c in copies:
                    c.start()
        else:
            work()
        for c in copies:
            c.wait()

    shape = jax.ShapeDtypeStruct
    if whole:
        outs = [shape((block, tokens), BF), shape((block, tokens), F32)]
    else:
        outs = [shape((stop, tokens), F32)]
    outs += [shape((v.shape[0], count), v.dtype) for v, _, _, count in loads]
    scratch = [
        pltpu.VMEM((lats, max(128, left)), BF),
        pltpu.SemaphoreType.DMA((2,)),
        pltpu.SemaphoreType.DMA((max(1, len(loads)),)),
    ]
    if whole:
        scratch.append(pltpu.VMEM((half, tokens), F32))
    args = (lat, after, in_hbm(dec), *heads) + ((done,) if ready else ()) + tuple(in_hbm(v) for v, *_ in loads)
    specs = [VMEM, ANY, HBM] + [VMEM] * (len(heads) + (ready > 0)) + [HBM] * len(loads)
    limit = 8 + lats * left * 2 // (1 << 20)
    return call(kernel, outs, scratch, args, specs, 2 * tokens * lats * (stop - ready), limit)


def part_of(rows, i):
    return pl.ds(i * (rows // PARTS), rows // PARTS)


def send_sum(oth, got):
    rows, tokens = oth.shape

    def kernel(oth_ref, got_ref, *out_refs):
        for i, out_ref in enumerate(out_refs):
            at = part_of(rows, i)
            out_ref[...] = (oth_ref[at, :] + got_ref[at, :].astype(F32)).astype(BF)

    outs = [jax.ShapeDtypeStruct((rows // PARTS, tokens), BF)] * PARTS
    return call(kernel, outs, [], (oth, got), [VMEM] * 2, TRANSFER, 4)


def next_send(oth, got):
    def kernel(oth_ref, got_ref, out_ref):
        out_ref[...] = (oth_ref[...] + got_ref[...].astype(F32)).astype(BF)

    return call(kernel, [jax.ShapeDtypeStruct(oth.shape, BF)], [], (oth, got), [VMEM] * 2, oth.size, 4)[0]


def layer_sum(i, own, got, back, q_own, q_got, q_back):
    rows, tokens = own.shape
    at = part_of(rows, i)

    def kernel(own_ref, got_ref, back_ref, qo_ref, qg_ref, qb_ref, sum_ref, out_ref):
        total = own_ref[at, :] + got_ref[at, :].astype(F32) + back_ref[...].astype(F32)
        sum_ref[...] = total

        @pl.when(whereabouts()[2] == 0)
        def _():
            extra = qo_ref[at, :] + qg_ref[at, :].astype(F32) + qb_ref[at, :].astype(F32)
            sum_ref[...] = sum_ref[...] + extra

        out_ref[...] = sum_ref[...].astype(BF)

    shape = jax.ShapeDtypeStruct
    outs = [shape((rows // PARTS, tokens), F32), shape((rows // PARTS, tokens), BF)]
    args = (own, got, back, q_own, q_got, q_back)
    return call(kernel, outs, [], args, [VMEM] * 6, TRANSFER, 5)


def next_sum(own, got, back):
    def kernel(own_ref, got_ref, back_ref, out_ref):
        out_ref[...] = (own_ref[...] + got_ref[...].astype(F32) + back_ref[...].astype(F32)).astype(BF)

    outs = [jax.ShapeDtypeStruct(own.shape, BF)]
    return call(kernel, outs, [], (own, got, back), [VMEM] * 3, own.size, 4)[0]


def recon_sum(own, got, extra, backs):
    rows, _ = own.shape

    def kernel(own_ref, got_ref, extra_ref, *refs):
        *back_refs, out_ref = refs
        from_first = whereabouts()[2] == 1
        for i, back_ref in enumerate(back_refs):
            at = part_of(rows, i)
            total = own_ref[at, :] + got_ref[at, :].astype(F32) + back_ref[...].astype(F32)
            extra = jnp.where(from_first, extra_ref[at, :].astype(F32), 0.0)
            out_ref[at, :] = (total + extra).astype(BF)

    outs = [jax.ShapeDtypeStruct(own.shape, BF)]
    args = (own, got, extra) + tuple(backs)
    return call(kernel, outs, [], args, [VMEM] * (3 + len(backs)), own.size, 5)[0]


def mix(i, target, other, frozen, gain):
    part, tokens = target.shape
    at = pl.ds(i * part, part)

    def kernel(t_ref, o_ref, f_ref, g_ref, out_ref):
        mixed = f_ref[at, :].astype(F32) + t_ref[...] + o_ref[...].astype(F32)
        gains = column_of(g_ref[...][None, :], tokens)
        out_ref[pl.ds(0, part), :] = (mixed * gains[i * part : (i + 1) * part, :]).astype(BF)
        squares = jnp.sum(mixed * mixed, axis=0, keepdims=True)
        high = squares.astype(BF).astype(F32)
        rest = squares - high
        mid = rest.astype(BF).astype(F32)
        low = rest - mid
        row = lax.broadcasted_iota(jnp.int32, (TAIL, tokens), 0)
        tail = jnp.where(row == 0, high, jnp.where(row == 1, mid, jnp.where(row == 2, low, 0.0)))
        out_ref[pl.ds(part, TAIL), :] = tail.astype(BF)

    outs = [jax.ShapeDtypeStruct((part + TAIL, tokens), BF)]
    return call(kernel, outs, [], (target, other, frozen, gain), [VMEM] * 4, TRANSFER, 5)[0]


def fold(keep, got, stays):
    count, piece, tokens = keep.shape

    def kernel(keep_ref, got_ref, *out_refs):
        for i, out_ref in enumerate(out_refs):
            out_ref[...] = (keep_ref[i] + got_ref[i].astype(F32)).astype(out_ref.dtype)

    outs = [jax.ShapeDtypeStruct((piece, tokens), F32 if stays and i == 0 else BF) for i in range(count)]
    return call(kernel, outs, [], (keep, got), [VMEM] * 2, count * piece * tokens, 6)


def last_sum(own, *others):
    def kernel(own_ref, *refs):
        *other_refs, out_ref = refs
        total = own_ref[...]
        for r in other_refs:
            total = total + r[...].astype(F32)
        out_ref[...] = total.astype(BF)

    outs = [jax.ShapeDtypeStruct(own.shape, BF)]
    return call(kernel, outs, [], (own,) + others, [VMEM] * (1 + len(others)), own.size, 4)[0]


def down_half(hidden_ref, wd_ref, snd_ref, keep_ref, yt, far):
    count, piece, _ = keep_ref.shape
    half = 2 * count * piece
    core, side, layer = whereabouts()
    col = pl.multiple_of((1 - layer if far else layer) * half, half)
    yt[...] = jnp.dot(hidden_ref[...], wd_ref[:, pl.ds(col, half)], preferred_element_type=F32).T
    for i in range(count):
        at = (side ^ i) * 2
        snd_ref[i] = yt[pl.ds(pl.multiple_of((at + 1 - core) * piece, piece), piece), :].astype(BF)
        keep_ref[i] = yt[pl.ds(pl.multiple_of((at + core) * piece, piece), piece), :]


def mlp_down(hidden, w_down, after, layers):
    tokens, units = hidden.shape
    feats = w_down.shape[1]
    piece = feats // (4 * layers)

    def kernel(hidden_ref, wd_ref, after_ref, snd_ref, keep_ref, yt):
        down_half(hidden_ref, wd_ref, snd_ref, keep_ref, yt, False)

    shape = jax.ShapeDtypeStruct
    outs = [shape((2, piece, tokens), BF), shape((2, piece, tokens), F32)]
    scratch = [pltpu.VMEM((feats // layers, tokens), F32)]
    args = (hidden, w_down, after)
    return call(kernel, outs, scratch, args, [VMEM, VMEM, ANY], tokens * units * feats, 6)


def mlp_half(owns, others, w_gate, w_up, first, extra, layers):
    part, tokens = owns[0].shape[0] - TAIL, owns[0].shape[1]
    width = part * PARTS
    half = 2 * width
    feats, units = w_gate.shape
    piece = feats // (4 * layers)

    def kernel(*rest):
        own_refs, other_refs, (wg_ref, wu_ref, *rest) = rest[:PARTS], rest[PARTS : 2 * PARTS], rest[2 * PARTS :]
        if first:
            lat_ref, g_ref, u_ref, sq_ref, lat_out, xg, sems = rest
            write = pltpu.make_async_copy(lat_ref, lat_out, sems.at[0])
            write.start()
        else:
            g_in, u_in, sq_in, wd_ref, hidden_ref, snd_ref, keep_ref, xg, yt = rest
        core, side, _ = whereabouts()
        row = side if first else 1 - side
        row = pl.multiple_of(row * half, half)

        def gather():
            squares = jnp.zeros((1, tokens), F32)
            for refs, c in ((own_refs, core), (other_refs, 1 - core)):
                for i, ref in enumerate(refs):
                    xg[pl.ds(pl.multiple_of(c * width + i * part, part), part), :] = ref[pl.ds(0, part), :]
                    squares += jnp.sum(ref[pl.ds(part, TAIL), :].astype(F32), axis=0, keepdims=True)
            gate = dot_cols(xg[...], wg_ref[pl.ds(row, half), :])
            up = dot_cols(xg[...], wu_ref[pl.ds(row, half), :])
            return squares, gate, up

        def work():
            squares, gate, up = gather()
            g_ref[...] = gate
            u_ref[...] = up
            sq_ref[...] = jnp.broadcast_to(squares, sq_ref.shape)

        if first:
            in_block(work)
            write.wait()
            return
        squares, gate, up = gather()
        total = squares + sq_in[0:1, :]
        scale = jnp.broadcast_to(lax.rsqrt(total / feats + 1e-06), (128, tokens)).T[:, 0:1]
        gate = scale * (gate + g_in[...])
        up = scale * (up + u_in[...])
        hidden_ref[...] = (jax.nn.gelu(gate, approximate=True) * up).astype(BF)
        down_half(hidden_ref, wd_ref, snd_ref, keep_ref, yt, True)

    shape = jax.ShapeDtypeStruct
    scratch = [pltpu.VMEM((half, tokens), BF)]
    out_specs = None
    if first:
        lat = extra[0]
        outs = [shape((tokens, units), F32), shape((tokens, units), F32), shape((8, tokens), F32)]
        outs += [shape(lat.shape, lat.dtype)]
        out_specs = [VMEM] * 3 + [HBM]
        scratch += [pltpu.SemaphoreType.DMA((1,))]
    else:
        outs = [shape((tokens, units), BF), shape((2, piece, tokens), BF), shape((2, piece, tokens), F32)]
        scratch += [pltpu.VMEM((feats // layers, tokens), F32)]
    args = (*owns, *others, w_gate, w_up) + extra
    flops = 4 * tokens * half * units + (0 if first else tokens * units * feats)
    return call(kernel, outs, scratch, args, [VMEM] * len(args), flops, 6 if first else 12, out_specs)


def blocked(
    resid_in, clt_gain, enc_w, enc_b, dec_same, dec_next, frozen_sum, mlp_gain, w_gate, w_up, w_down
):
    return blocked_steps(
        resid_in, clt_gain, enc_w, enc_b, dec_same, dec_next, frozen_sum, mlp_gain, w_gate, w_up, w_down
    )


def blocked_steps(
    resid_in, clt_gain, enc_w, enc_b, dec_same, dec_next, frozen_sum, mlp_gain, w_gate, w_up, w_down
):
    layers = lax.axis_size("layer")
    both = ("layer", "latent")

    def partner(v):
        return lax.ppermute(v, "latent", [(i, i ^ 1) for i in range(4)])

    def across(v):
        return lax.ppermute(v, "latent", [(i, i ^ 2) for i in range(4)])

    def other_layer(v):
        return lax.ppermute(v, "layer", [(0, 1), (1, 0)])

    own = resid_in[0].T
    far = across(own)
    near = partner(own)
    parts = encode_first(own, near, clt_gain, enc_b, enc_w[0])
    far_near = partner(far)
    acc, sq, gains, bias, rest = parts
    half = dec_next.shape[1] // 2
    cut = half // 256 * 128
    few, many = cut // 2, half - cut // 2
    acc, sq, far_2 = encode_more(far, acc, sq, gains, rest, False, [(dec_next, True, cut, half - cut)])
    loads = [(dec_next, True, 0, cut), (dec_next, False, 0, few)]
    lat, far_1, near_1 = encode_more(far_near, acc, sq, gains, rest, True, loads, bias, enc_w.shape[1])

    def to_partner(snd, pairs):
        return lax.ppermute(snd, both, [(i, i ^ 1) for i in pairs])

    def to_chip(sent, pairs):
        return lax.ppermute(sent, both, [(i, i ^ 2) for i in pairs])

    same, frozen = dec_same[0], frozen_sum.T
    every = range(8)
    loads = [(dec_next, False, few, many)]
    snd, oth, near_2 = decode(lat, None, [far_1, far_2], dec_next, lat, True, True, half, loads)
    got = to_partner(snd, every)
    loads = [(same, True, 0, many)]
    snd_near, q_own, head = decode(lat, None, [near_1, near_2], dec_next, snd, False, True, half, loads)
    q_back = to_chip(next_send(oth, got), every)
    q_got = to_partner(snd_near, every)
    loads = [(same, False, 0, cut + few), (frozen, None, 0, frozen.shape[1])]
    snd, oth, head, frozen = decode(lat, None, [head], same, snd_near, True, False, half, loads)
    got = to_partner(snd, every)
    loads = [(same, False, cut + few, many - cut)]
    done, head = decode(lat, None, [head], same, snd, False, False, cut + few, loads)
    sents = send_sum(oth, got)
    backs = [to_chip(sent, every) for sent in sents]
    snd_near, own = decode(lat, done, [head], same, done, False, False, half, [])
    got = to_partner(snd_near, every)
    normed = []
    for i, back in enumerate(backs):
        total, sent = layer_sum(i, own, got, back, q_own, q_got, q_back)
        normed.append(mix(i, total, other_layer(sent), frozen, mlp_gain))
    w_gate, w_up, w_down = resident(w_gate), resident(w_up), resident(w_down)
    n_near = [partner(v) for v in normed]
    n_far = [across(v) for v in normed]
    q_here = other_layer(next_sum(q_own, q_got, q_back))
    recon = recon_sum(own, got, q_here, backs)
    g, u, nsq, lat_out = mlp_half(normed, n_near, w_gate, w_up, True, (lat,), layers)
    n_far_near = [partner(v) for v in n_far]
    hidden, snd, keep = mlp_half(n_far, n_far_near, w_gate, w_up, False, (g, u, nsq, w_down), layers)
    got = partner(snd)
    snd, near_keep = mlp_down(hidden, w_down, snd, layers)
    near_got = partner(snd)
    to_x, to_d = fold(keep, got, False)
    r_d = lax.ppermute(to_d, both, [(i, i ^ 6) for i in range(8)])
    r_x = other_layer(to_x)
    kept, to_y = fold(near_keep, near_got, True)
    r_y = across(to_y)
    out = last_sum(kept, r_x, r_y, r_d)
    return (lat_out[None], recon.T[None], out.T)


def passed_along(block, axis, distance):
    devices = range(lax.axis_size(axis))
    route = [(i - distance, i) for i in devices if i - distance in devices]
    return lax.ppermute(block, axis, route)


def swapped_with(value, axis, stride):
    mask = 2**stride
    pairs = [(source, source ^ mask) for source in range(lax.axis_size(axis))]
    return lax.ppermute(value, axis, pairs)


def general(
    resid_in, clt_gain, enc_w, enc_b, dec_same, dec_next, frozen_sum, mlp_gain, w_gate, w_up, w_down
):
    own_rows = resid_in[0]
    feats = enc_w.shape[1]
    own_values = own_rows.astype(F32)
    squares = lax.psum(jnp.sum(own_values * own_values, axis=1, keepdims=True), "latent")
    gated = (lax.all_gather(own_rows, "latent", axis=1, tiled=True).astype(F32) * clt_gain[0]).astype(BF)
    projected = jnp.dot(gated, enc_w[0], preferred_element_type=F32)
    inv_scale = lax.rsqrt(squares / feats + 1e-06)
    lat_act = jnp.maximum(inv_scale * projected + enc_b[0], 0.0).astype(BF)
    is_first = lax.axis_index("layer") == 0
    own_term = jnp.dot(lat_act, dec_same[0], preferred_element_type=F32)
    arrived = passed_along(lat_act, "layer", 1)
    target_term = own_term + jnp.dot(arrived, dec_next, preferred_element_type=F32)
    own_sum = lax.psum_scatter(target_term, "latent", scatter_dimension=1, tiled=True)
    other_sum = swapped_with(own_sum, "layer", 0)
    recon_zero = jnp.where(is_first, own_sum, other_sum)
    recon_one = jnp.where(is_first, other_sum, own_sum)
    recon = own_sum.astype(BF)[None]
    mixed = frozen_sum.astype(F32) + recon_zero + recon_one
    normed = (mixed * mlp_gain).astype(BF)
    mixed_squares = lax.psum(jnp.sum(mixed * mixed, axis=1, keepdims=True), "latent")
    rows = lax.all_gather(normed, "latent", axis=1, tiled=True)
    gate_raw = jnp.dot(rows, w_gate, preferred_element_type=F32)
    up_raw = jnp.dot(rows, w_up, preferred_element_type=F32)
    row_scale = lax.rsqrt(mixed_squares / feats + 1e-06)
    hidden = (jax.nn.gelu(row_scale * gate_raw, approximate=True) * (row_scale * up_raw)).astype(BF)
    partials = jnp.dot(hidden, w_down, preferred_element_type=F32)
    mlp_out = lax.psum_scatter(
        partials, ("layer", "latent"), scatter_dimension=1, tiled=True
    ).astype(BF)
    return (lat_act[None], recon, mlp_out)


def solution(mesh):
    in_specs = (
        P("layer", "token", "latent"),
        P("layer", None),
        P("layer", None, "latent"),
        P("layer", "latent"),
        P("layer", "latent", None),
        P("latent", None),
        P("token", "latent"),
        P("latent"),
        P(None, ("layer", "latent")),
        P(None, ("layer", "latent")),
        P(("layer", "latent"), None),
    )
    out_specs = (
        P("layer", "token", "latent"),
        P("layer", "token", "latent"),
        P("token", ("layer", "latent")),
    )
    small = mesh.shape["layer"] == 2 and mesh.shape["latent"] == 4
    return jax.shard_map(
        blocked if small else general, mesh=mesh, in_specs=in_specs, out_specs=out_specs, check_vma=False
    )
```

```python
import functools

import jax
import jax.numpy as jnp
from jax import lax
from jax.experimental import pallas as pl
from jax.experimental.pallas import tpu as pltpu
from jax.sharding import PartitionSpec as P


BF = jnp.bfloat16
F32 = jnp.float32
VMEM = pl.BlockSpec(memory_space=pltpu.VMEM)
HBM = pl.BlockSpec(memory_space=pltpu.HBM)
ANY = pl.BlockSpec(memory_space=pl.ANY)
TAIL = 16
PARTS = 3
TRANSFER = 3 << 30


def dot_cols(x_km, w_kn):
    return lax.dot_general(x_km, w_kn, (((0,), (0,)), ((), ())), preferred_element_type=F32)


def whereabouts():
    place = lax.axis_index("latent")
    return place & 1, place >> 1, lax.axis_index("layer")


def in_block(work):
    pl.when(lax.axis_index("latent") >= 0)(work)


def column_of(row, width):
    n = row.shape[1]
    block = jnp.broadcast_to(row, (128, n)).T
    return jnp.concatenate([block] * (width // 128), axis=1)


def call(kernel, out_shapes, scratch, args, specs, flops, limit, out_specs=None):
    return pl.pallas_call(
        kernel,
        out_shape=out_shapes,
        in_specs=specs,
        out_specs=[VMEM] * len(out_shapes) if out_specs is None else out_specs,
        scratch_shapes=scratch,
        cost_estimate=pl.CostEstimate(flops=flops, transcendentals=0, bytes_accessed=0),
        compiler_params=pltpu.CompilerParams(vmem_limit_bytes=limit << 20),
    )(*args)


def in_hbm(array):
    return pltpu.with_memory_space_constraint(array, pltpu.HBM)


def resident(weights):
    return pltpu.with_memory_space_constraint(weights, pltpu.VMEM)


def pick(total, wanted):
    size = wanted - wanted % 128
    while size > 128 and total % size:
        size -= 128
    return size if total % size == 0 else total


def encode_first(own, other, gain, bias, enc):
    width, tokens = own.shape
    _, lats = enc.shape
    half = 2 * width
    tn = pick(lats, 1024)
    steps = lats // tn
    ahead = 3

    def kernel(
        own_ref, other_ref, gain_ref, bias_ref, enc_ref,
        acc_ref, sq_ref, gain_out, bias_out, rest_ref,
        xg, xown, gbuf, grest, wbuf, sems, small
    ):
        core, side, _ = whereabouts()
        mine = pl.multiple_of(side * half, half)
        others = pl.multiple_of((1 - side) * half, half)
        loads = [
            pltpu.make_async_copy(own_ref, xown, small.at[0]),
            pltpu.make_async_copy(gain_ref.at[:, pl.ds(mine, half)], gbuf, small.at[1]),
        ]
        later = [
            pltpu.make_async_copy(gain_ref.at[:, pl.ds(others, half)], grest, small.at[2]),
            pltpu.make_async_copy(bias_ref, bias_out, small.at[3]),
        ]

        def weights(j):
            cols = pl.ds(j % steps * tn, tn)
            if j < steps:
                return pltpu.make_async_copy(enc_ref.at[pl.ds(mine, half), cols], wbuf.at[:, cols], sems.at[j])
            return pltpu.make_async_copy(enc_ref.at[pl.ds(others, half), cols], rest_ref.at[:, cols], sems.at[j])

        for c in loads:
            c.start()
        for j in range(ahead):
            weights(j).start()
        for c in later:
            c.start()
        for c in loads:
            c.wait()

        def gather():
            xg[pl.ds(pl.multiple_of(core * width, width), width), :] = xown[...]
            xg[pl.ds(pl.multiple_of((1 - core) * width, width), width), :] = other_ref[...]
            values = xg[...].astype(F32)
            squares = jnp.sum(values * values, axis=0, keepdims=True)
            xg[...] = (values * column_of(gbuf[...], tokens)).astype(BF)
            sq_ref[...] = jnp.broadcast_to(squares, sq_ref.shape)

        def apply(j):
            cols = pl.ds(j * tn, tn)
            acc_ref[:, cols] = dot_cols(xg[...], wbuf[:, cols])

        def spread():
            gain_out[...] = column_of(grest[...], tokens)

        in_block(gather)
        for j in range(2 * steps):
            if j == steps:
                for c in later:
                    c.wait()
                in_block(spread)
            weights(j).wait()
            if j + ahead < 2 * steps:
                weights(j + ahead).start()
            if j < steps:
                in_block(functools.partial(apply, j))

    shape = jax.ShapeDtypeStruct
    outs = [
        shape((tokens, lats), F32),
        shape((8, tokens), F32),
        shape((half, tokens), F32),
        shape((1, lats), F32),
        shape((half, lats), BF),
    ]
    scratch = [
        pltpu.VMEM((half, tokens), BF),
        pltpu.VMEM((width, tokens), BF),
        pltpu.VMEM((1, half), F32),
        pltpu.VMEM((1, half), F32),
        pltpu.VMEM((half, lats), BF),
        pltpu.SemaphoreType.DMA((2 * steps,)),
        pltpu.SemaphoreType.DMA((4,)),
    ]
    specs = [HBM, VMEM, HBM, HBM, HBM]
    return call(
        kernel,
        outs,
        scratch,
        (in_hbm(own), other, in_hbm(gain), in_hbm(bias), in_hbm(enc)),
        specs,
        8 * tokens * half * lats,
        16,
    )


def encode_more(block, acc, sq, gain, rest, near, loads, bias=None, feats=0):
    width, tokens = block.shape
    lats = rest.shape[1]
    tn = pick(lats, 1024)
    count = len(loads)
    last = bias is not None

    def kernel(block_ref, acc_ref, sq_ref, gain_ref, rest_ref, *refs):
        load_refs, refs = refs[:count], refs[count:]
        if last:
            bias_ref, out_ref, *refs = refs
        else:
            out_ref, sq_out, *refs = refs
        loaded_refs, (xg, sems, *scale_refs) = refs[:count], refs[count:]
        copies = [
            pltpu.make_async_copy(columns(source, load), target, sems.at[i])
            for i, (source, target, load) in enumerate(zip(load_refs, loaded_refs, loads))
        ]
        for c in copies:
            c.start()
        core = whereabouts()[0]
        row = pl.multiple_of((1 - core if near else core) * width, width)

        def work():
            values = block_ref[...].astype(F32)
            squares = jnp.sum(values * values, axis=0, keepdims=True) + sq_ref[0:1, :]
            xg[...] = (values * gain_ref[pl.ds(row, width), :]).astype(BF)
            if last:
                scale_refs[0][...] = jnp.broadcast_to(lax.rsqrt(squares / feats + 1e-06), (128, tokens)).T
            else:
                sq_out[...] = jnp.broadcast_to(squares, sq_out.shape)
            for j in range(lats // tn):
                cols = pl.ds(j * tn, tn)
                total = dot_cols(xg[...], rest_ref[pl.ds(row, width), cols]) + acc_ref[:, cols]
                if last:
                    out_ref[:, cols] = jnp.maximum(scale_refs[0][:, 0:1] * total + bias_ref[:, cols], 0.0).astype(BF)
                else:
                    out_ref[:, cols] = total

        in_block(work)
        for c in copies:
            c.wait()

    shape = jax.ShapeDtypeStruct
    heads = [shape((v.shape[0], cols), v.dtype) for v, _, _, cols in loads]
    scratch = [pltpu.VMEM((width, tokens), BF), pltpu.SemaphoreType.DMA((count,))]
    args = (block, acc, sq, gain, rest) + tuple(in_hbm(v) for v, *_ in loads)
    specs = [VMEM] * 5 + [HBM] * count
    if last:
        args, specs = args + (bias,), specs + [VMEM]
        outs = [shape((tokens, lats), BF)] + heads
        scratch += [pltpu.VMEM((tokens, 128), F32)]
    else:
        outs = [shape((tokens, lats), F32), shape((8, tokens), F32)] + heads
    return call(kernel, outs, scratch, args, specs, 2 * tokens * width * lats, 8)


def columns(ref, load):
    _, far, at, count = load
    if far is None:
        return ref
    side = whereabouts()[1]
    base = (1 - side if far else side) * (ref.shape[1] // 2) + at
    return ref.at[:, pl.ds(pl.multiple_of(base, 128), count)]


def decode(lat, done, heads, dec, after, far, only_first, stop, loads):
    tokens, lats = lat.shape
    half = dec.shape[1] // 2
    block = half // 2
    whole = stop == half
    ready = 0 if done is None else done.shape[0]
    widths = [h.shape[1] for h in heads]
    loaded = ready + sum(widths)
    left = stop - loaded
    rows_of = lats // 2

    def kernel(lat_ref, after_ref, dec_ref, *rest):
        head_refs, rest = rest[: len(heads)], rest[len(heads) :]
        if ready:
            done_ref, *rest = rest
        load_refs, rest = rest[: len(loads)], rest[len(loads) :]
        if whole:
            snd_ref, keep_ref, *rest = rest
        else:
            sums_ref, *rest = rest
        loaded_refs, rest = rest[: len(loads)], rest[len(loads) :]
        wbuf, wsems, sems, *rest = rest
        yt = rest[0] if whole else sums_ref
        copies = [
            pltpu.make_async_copy(columns(source, load), target, sems.at[i])
            for i, (source, target, load) in enumerate(zip(load_refs, loaded_refs, loads))
        ]
        core, _, layer = whereabouts()
        weights = columns(dec_ref, (None, far, loaded, left)) if left else None

        def fetch(k):
            rows = pl.ds(k * rows_of, rows_of)
            return pltpu.make_async_copy(weights.at[rows, :], wbuf.at[rows, :], wsems.at[k])

        def apply(at, size, weights_of):
            yt[pl.ds(at, size), :] = jnp.dot(lat_ref[...], weights_of[...], preferred_element_type=F32).T

        def bring():
            yt[pl.ds(0, ready), :] = done_ref[...]

        def share():
            snd_ref[...] = yt[pl.ds(pl.multiple_of((1 - core) * block, block), block), :].astype(BF)
            keep_ref[...] = yt[pl.ds(pl.multiple_of(core * block, block), block), :]

        def work():
            if left:
                for k in range(2):
                    fetch(k).start()
            for c in copies:
                c.start()
            if ready:
                in_block(bring)
            at = ready
            for i, width in enumerate(widths):
                in_block(functools.partial(apply, at, width, head_refs[i]))
                at += width
            if left:
                for k in range(2):
                    fetch(k).wait()
                in_block(functools.partial(apply, at, left, wbuf))
            if whole:
                in_block(share)

        if only_first:
            pl.when(layer == 0)(work)

            @pl.when(layer != 0)
            def _():
                for c in copies:
                    c.start()
        else:
            work()
        for c in copies:
            c.wait()

    shape = jax.ShapeDtypeStruct
    if whole:
        outs = [shape((block, tokens), BF), shape((block, tokens), F32)]
    else:
        outs = [shape((stop, tokens), F32)]
    outs += [shape((v.shape[0], count), v.dtype) for v, _, _, count in loads]
    scratch = [
        pltpu.VMEM((lats, max(128, left)), BF),
        pltpu.SemaphoreType.DMA((2,)),
        pltpu.SemaphoreType.DMA((max(1, len(loads)),)),
    ]
    if whole:
        scratch.append(pltpu.VMEM((half, tokens), F32))
    args = (lat, after, in_hbm(dec), *heads) + ((done,) if ready else ()) + tuple(in_hbm(v) for v, *_ in loads)
    specs = [VMEM, ANY, HBM] + [VMEM] * (len(heads) + (ready > 0)) + [HBM] * len(loads)
    limit = 8 + lats * left * 2 // (1 << 20)
    return call(kernel, outs, scratch, args, specs, 2 * tokens * lats * (stop - ready), limit)


def part_of(rows, i):
    return pl.ds(i * (rows // PARTS), rows // PARTS)


def send_sum(oth, got):
    rows, tokens = oth.shape

    def kernel(oth_ref, got_ref, *out_refs):
        for i, out_ref in enumerate(out_refs):
            at = part_of(rows, i)
            out_ref[...] = (oth_ref[at, :] + got_ref[at, :].astype(F32)).astype(BF)

    outs = [jax.ShapeDtypeStruct((rows // PARTS, tokens), BF)] * PARTS
    return call(kernel, outs, [], (oth, got), [VMEM] * 2, TRANSFER, 4)


def next_send(oth, got):
    def kernel(oth_ref, got_ref, out_ref):
        out_ref[...] = (oth_ref[...] + got_ref[...].astype(F32)).astype(BF)

    return call(kernel, [jax.ShapeDtypeStruct(oth.shape, BF)], [], (oth, got), [VMEM] * 2, oth.size, 4)[0]


def layer_sum(i, own, got, back, q_own, q_got, q_back):
    rows, tokens = own.shape
    at = part_of(rows, i)

    def kernel(own_ref, got_ref, back_ref, qo_ref, qg_ref, qb_ref, sum_ref, out_ref):
        total = own_ref[at, :] + got_ref[at, :].astype(F32) + back_ref[...].astype(F32)
        sum_ref[...] = total

        @pl.when(whereabouts()[2] == 0)
        def _():
            extra = qo_ref[at, :] + qg_ref[at, :].astype(F32) + qb_ref[at, :].astype(F32)
            sum_ref[...] = sum_ref[...] + extra

        out_ref[...] = sum_ref[...].astype(BF)

    shape = jax.ShapeDtypeStruct
    outs = [shape((rows // PARTS, tokens), F32), shape((rows // PARTS, tokens), BF)]
    args = (own, got, back, q_own, q_got, q_back)
    return call(kernel, outs, [], args, [VMEM] * 6, TRANSFER, 5)


def next_sum(own, got, back):
    def kernel(own_ref, got_ref, back_ref, out_ref):
        out_ref[...] = (own_ref[...] + got_ref[...].astype(F32) + back_ref[...].astype(F32)).astype(BF)

    outs = [jax.ShapeDtypeStruct(own.shape, BF)]
    return call(kernel, outs, [], (own, got, back), [VMEM] * 3, own.size, 4)[0]


def recon_sum(own, got, extra, backs):
    rows, _ = own.shape

    def kernel(own_ref, got_ref, extra_ref, *refs):
        *back_refs, out_ref = refs
        from_first = whereabouts()[2] == 1
        for i, back_ref in enumerate(back_refs):
            at = part_of(rows, i)
            total = own_ref[at, :] + got_ref[at, :].astype(F32) + back_ref[...].astype(F32)
            extra = jnp.where(from_first, extra_ref[at, :].astype(F32), 0.0)
            out_ref[at, :] = (total + extra).astype(BF)

    outs = [jax.ShapeDtypeStruct(own.shape, BF)]
    args = (own, got, extra) + tuple(backs)
    return call(kernel, outs, [], args, [VMEM] * (3 + len(backs)), own.size, 5)[0]


def mix(i, target, other, frozen, gain):
    part, tokens = target.shape
    at = pl.ds(i * part, part)

    def kernel(t_ref, o_ref, f_ref, g_ref, out_ref):
        mixed = f_ref[at, :].astype(F32) + t_ref[...] + o_ref[...].astype(F32)
        gains = column_of(g_ref[...][None, :], tokens)
        out_ref[pl.ds(0, part), :] = (mixed * gains[i * part : (i + 1) * part, :]).astype(BF)
        squares = jnp.sum(mixed * mixed, axis=0, keepdims=True)
        high = squares.astype(BF).astype(F32)
        rest = squares - high
        mid = rest.astype(BF).astype(F32)
        low = rest - mid
        row = lax.broadcasted_iota(jnp.int32, (TAIL, tokens), 0)
        tail = jnp.where(row == 0, high, jnp.where(row == 1, mid, jnp.where(row == 2, low, 0.0)))
        out_ref[pl.ds(part, TAIL), :] = tail.astype(BF)

    outs = [jax.ShapeDtypeStruct((part + TAIL, tokens), BF)]
    return call(kernel, outs, [], (target, other, frozen, gain), [VMEM] * 4, TRANSFER, 5)[0]


def fold(keep, got, stays):
    count, piece, tokens = keep.shape

    def kernel(keep_ref, got_ref, *out_refs):
        for i, out_ref in enumerate(out_refs):
            out_ref[...] = (keep_ref[i] + got_ref[i].astype(F32)).astype(out_ref.dtype)

    outs = [jax.ShapeDtypeStruct((piece, tokens), F32 if stays and i == 0 else BF) for i in range(count)]
    return call(kernel, outs, [], (keep, got), [VMEM] * 2, count * piece * tokens, 6)


def last_sum(own, *others):
    def kernel(own_ref, *refs):
        *other_refs, out_ref = refs
        total = own_ref[...]
        for r in other_refs:
            total = total + r[...].astype(F32)
        out_ref[...] = total.astype(BF)

    outs = [jax.ShapeDtypeStruct(own.shape, BF)]
    return call(kernel, outs, [], (own,) + others, [VMEM] * (1 + len(others)), own.size, 4)[0]


def down_half(hidden_ref, wd_ref, snd_ref, keep_ref, yt, far):
    count, piece, _ = keep_ref.shape
    half = 2 * count * piece
    core, side, layer = whereabouts()
    col = pl.multiple_of((1 - layer if far else layer) * half, half)
    yt[...] = jnp.dot(hidden_ref[...], wd_ref[:, pl.ds(col, half)], preferred_element_type=F32).T
    for i in range(count):
        at = (side ^ i) * 2
        snd_ref[i] = yt[pl.ds(pl.multiple_of((at + 1 - core) * piece, piece), piece), :].astype(BF)
        keep_ref[i] = yt[pl.ds(pl.multiple_of((at + core) * piece, piece), piece), :]


def mlp_down(hidden, w_down, after, layers):
    tokens, units = hidden.shape
    feats = w_down.shape[1]
    piece = feats // (4 * layers)

    def kernel(hidden_ref, wd_ref, after_ref, snd_ref, keep_ref, yt):
        down_half(hidden_ref, wd_ref, snd_ref, keep_ref, yt, False)

    shape = jax.ShapeDtypeStruct
    outs = [shape((2, piece, tokens), BF), shape((2, piece, tokens), F32)]
    scratch = [pltpu.VMEM((feats // layers, tokens), F32)]
    args = (hidden, w_down, after)
    return call(kernel, outs, scratch, args, [VMEM, VMEM, ANY], tokens * units * feats, 6)


def mlp_half(owns, others, w_gate, w_up, first, extra, layers):
    part, tokens = owns[0].shape[0] - TAIL, owns[0].shape[1]
    width = part * PARTS
    half = 2 * width
    feats, units = w_gate.shape
    piece = feats // (4 * layers)

    def kernel(*rest):
        own_refs, other_refs, (wg_ref, wu_ref, *rest) = rest[:PARTS], rest[PARTS : 2 * PARTS], rest[2 * PARTS :]
        if first:
            lat_ref, g_ref, u_ref, sq_ref, lat_out, xg, sems = rest
            write = pltpu.make_async_copy(lat_ref, lat_out, sems.at[0])
            write.start()
        else:
            g_in, u_in, sq_in, wd_ref, hidden_ref, snd_ref, keep_ref, xg, yt = rest
        core, side, _ = whereabouts()
        row = side if first else 1 - side
        row = pl.multiple_of(row * half, half)

        def gather():
            squares = jnp.zeros((1, tokens), F32)
            for refs, c in ((own_refs, core), (other_refs, 1 - core)):
                for i, ref in enumerate(refs):
                    xg[pl.ds(pl.multiple_of(c * width + i * part, part), part), :] = ref[pl.ds(0, part), :]
                    squares += jnp.sum(ref[pl.ds(part, TAIL), :].astype(F32), axis=0, keepdims=True)
            gate = dot_cols(xg[...], wg_ref[pl.ds(row, half), :])
            up = dot_cols(xg[...], wu_ref[pl.ds(row, half), :])
            return squares, gate, up

        def work():
            squares, gate, up = gather()
            g_ref[...] = gate
            u_ref[...] = up
            sq_ref[...] = jnp.broadcast_to(squares, sq_ref.shape)

        if first:
            in_block(work)
            write.wait()
            return
        squares, gate, up = gather()
        total = squares + sq_in[0:1, :]
        scale = jnp.broadcast_to(lax.rsqrt(total / feats + 1e-06), (128, tokens)).T[:, 0:1]
        gate = scale * (gate + g_in[...])
        up = scale * (up + u_in[...])
        hidden_ref[...] = (jax.nn.gelu(gate, approximate=True) * up).astype(BF)
        down_half(hidden_ref, wd_ref, snd_ref, keep_ref, yt, True)

    shape = jax.ShapeDtypeStruct
    scratch = [pltpu.VMEM((half, tokens), BF)]
    out_specs = None
    if first:
        lat = extra[0]
        outs = [shape((tokens, units), F32), shape((tokens, units), F32), shape((8, tokens), F32)]
        outs += [shape(lat.shape, lat.dtype)]
        out_specs = [VMEM] * 3 + [HBM]
        scratch += [pltpu.SemaphoreType.DMA((1,))]
    else:
        outs = [shape((tokens, units), BF), shape((2, piece, tokens), BF), shape((2, piece, tokens), F32)]
        scratch += [pltpu.VMEM((feats // layers, tokens), F32)]
    args = (*owns, *others, w_gate, w_up) + extra
    flops = 4 * tokens * half * units + (0 if first else tokens * units * feats)
    return call(kernel, outs, scratch, args, [VMEM] * len(args), flops, 6 if first else 12, out_specs)


def blocked(
    resid_in, clt_gain, enc_w, enc_b, dec_same, dec_next, frozen_sum, mlp_gain, w_gate, w_up, w_down
):
    return blocked_steps(
        resid_in, clt_gain, enc_w, enc_b, dec_same, dec_next, frozen_sum, mlp_gain, w_gate, w_up, w_down
    )


def blocked_steps(
    resid_in, clt_gain, enc_w, enc_b, dec_same, dec_next, frozen_sum, mlp_gain, w_gate, w_up, w_down
):
    layers = lax.axis_size("layer")
    both = ("layer", "latent")

    def partner(v):
        return lax.ppermute(v, "latent", [(i, i ^ 1) for i in range(4)])

    def across(v):
        return lax.ppermute(v, "latent", [(i, i ^ 2) for i in range(4)])

    def other_layer(v):
        return lax.ppermute(v, "layer", [(0, 1), (1, 0)])

    own = resid_in[0].T
    far = across(own)
    near = partner(own)
    parts = encode_first(own, near, clt_gain, enc_b, enc_w[0])
    far_near = partner(far)
    acc, sq, gains, bias, rest = parts
    half = dec_next.shape[1] // 2
    cut = half // 256 * 128
    few, many = cut // 2, half - cut // 2
    acc, sq, far_2 = encode_more(far, acc, sq, gains, rest, False, [(dec_next, True, cut, half - cut)])
    loads = [(dec_next, True, 0, cut), (dec_next, False, 0, few)]
    lat, far_1, near_1 = encode_more(far_near, acc, sq, gains, rest, True, loads, bias, enc_w.shape[1])

    def to_partner(snd, pairs):
        return lax.ppermute(snd, both, [(i, i ^ 1) for i in pairs])

    def to_chip(sent, pairs):
        return lax.ppermute(sent, both, [(i, i ^ 2) for i in pairs])

    same, frozen = dec_same[0], frozen_sum.T
    every = range(8)
    loads = [(dec_next, False, few, many)]
    snd, oth, near_2 = decode(lat, None, [far_1, far_2], dec_next, lat, True, True, half, loads)
    got = to_partner(snd, every)
    loads = [(same, True, 0, many)]
    snd_near, q_own, head = decode(lat, None, [near_1, near_2], dec_next, snd, False, True, half, loads)
    q_back = to_chip(next_send(oth, got), every)
    q_got = to_partner(snd_near, every)
    loads = [(same, False, 0, cut + few)]
    snd, oth, head = decode(lat, None, [head], same, snd_near, True, False, half, loads)
    got = to_partner(snd, every)
    loads = [(same, False, cut + few, many - cut)]
    done, head = decode(lat, None, [head], same, snd, False, False, cut + few, loads)
    sents = send_sum(oth, got)
    backs = [to_chip(sent, every) for sent in sents]
    loads = [(frozen, None, 0, frozen.shape[1])]
    snd_near, own, frozen = decode(lat, done, [head], same, done, False, False, half, loads)
    got = to_partner(snd_near, every)
    normed = []
    for i, back in enumerate(backs):
        total, sent = layer_sum(i, own, got, back, q_own, q_got, q_back)
        normed.append(mix(i, total, other_layer(sent), frozen, mlp_gain))
    w_gate, w_up, w_down = resident(w_gate), resident(w_up), resident(w_down)
    n_near = [partner(v) for v in normed]
    n_far = [across(v) for v in normed]
    q_here = other_layer(next_sum(q_own, q_got, q_back))
    recon = recon_sum(own, got, q_here, backs)
    g, u, nsq, lat_out = mlp_half(normed, n_near, w_gate, w_up, True, (lat,), layers)
    n_far_near = [partner(v) for v in n_far]
    hidden, snd, keep = mlp_half(n_far, n_far_near, w_gate, w_up, False, (g, u, nsq, w_down), layers)
    got = partner(snd)
    snd, near_keep = mlp_down(hidden, w_down, snd, layers)
    near_got = partner(snd)
    to_x, to_d = fold(keep, got, False)
    r_d = lax.ppermute(to_d, both, [(i, i ^ 6) for i in range(8)])
    r_x = other_layer(to_x)
    kept, to_y = fold(near_keep, near_got, True)
    r_y = across(to_y)
    out = last_sum(kept, r_x, r_y, r_d)
    return (lat_out[None], recon.T[None], out.T)


def passed_along(block, axis, distance):
    devices = range(lax.axis_size(axis))
    route = [(i - distance, i) for i in devices if i - distance in devices]
    return lax.ppermute(block, axis, route)


def swapped_with(value, axis, stride):
    mask = 2**stride
    pairs = [(source, source ^ mask) for source in range(lax.axis_size(axis))]
    return lax.ppermute(value, axis, pairs)


def general(
    resid_in, clt_gain, enc_w, enc_b, dec_same, dec_next, frozen_sum, mlp_gain, w_gate, w_up, w_down
):
    own_rows = resid_in[0]
    feats = enc_w.shape[1]
    own_values = own_rows.astype(F32)
    squares = lax.psum(jnp.sum(own_values * own_values, axis=1, keepdims=True), "latent")
    gated = (lax.all_gather(own_rows, "latent", axis=1, tiled=True).astype(F32) * clt_gain[0]).astype(BF)
    projected = jnp.dot(gated, enc_w[0], preferred_element_type=F32)
    inv_scale = lax.rsqrt(squares / feats + 1e-06)
    lat_act = jnp.maximum(inv_scale * projected + enc_b[0], 0.0).astype(BF)
    is_first = lax.axis_index("layer") == 0
    own_term = jnp.dot(lat_act, dec_same[0], preferred_element_type=F32)
    arrived = passed_along(lat_act, "layer", 1)
    target_term = own_term + jnp.dot(arrived, dec_next, preferred_element_type=F32)
    own_sum = lax.psum_scatter(target_term, "latent", scatter_dimension=1, tiled=True)
    other_sum = swapped_with(own_sum, "layer", 0)
    recon_zero = jnp.where(is_first, own_sum, other_sum)
    recon_one = jnp.where(is_first, other_sum, own_sum)
    recon = own_sum.astype(BF)[None]
    mixed = frozen_sum.astype(F32) + recon_zero + recon_one
    normed = (mixed * mlp_gain).astype(BF)
    mixed_squares = lax.psum(jnp.sum(mixed * mixed, axis=1, keepdims=True), "latent")
    rows = lax.all_gather(normed, "latent", axis=1, tiled=True)
    gate_raw = jnp.dot(rows, w_gate, preferred_element_type=F32)
    up_raw = jnp.dot(rows, w_up, preferred_element_type=F32)
    row_scale = lax.rsqrt(mixed_squares / feats + 1e-06)
    hidden = (jax.nn.gelu(row_scale * gate_raw, approximate=True) * (row_scale * up_raw)).astype(BF)
    partials = jnp.dot(hidden, w_down, preferred_element_type=F32)
    mlp_out = lax.psum_scatter(
        partials, ("layer", "latent"), scatter_dimension=1, tiled=True
    ).astype(BF)
    return (lat_act[None], recon, mlp_out)


def solution(mesh):
    in_specs = (
        P("layer", "token", "latent"),
        P("layer", None),
        P("layer", None, "latent"),
        P("layer", "latent"),
        P("layer", "latent", None),
        P("latent", None),
        P("token", "latent"),
        P("latent"),
        P(None, ("layer", "latent")),
        P(None, ("layer", "latent")),
        P(("layer", "latent"), None),
    )
    out_specs = (
        P("layer", "token", "latent"),
        P("layer", "token", "latent"),
        P("token", ("layer", "latent")),
    )
    small = mesh.shape["layer"] == 2 and mesh.shape["latent"] == 4
    return jax.shard_map(
        blocked if small else general, mesh=mesh, in_specs=in_specs, out_specs=out_specs, check_vma=False
    )
```
